32 devices in a mesh: scen: 8 (over y, x, core), bldg: 4 (over z).
Axes of the slice: x: 2, y: 2, z: 4, core: 2. Of those that a mesh axis runs over, the one named last changes fastest.
Arguments:
- demand: float32 [128, 1024, 96], P('scen', 'bldg'), may hold values from -6 to 6
- tariff: float32 [128, 96], P('scen'), may hold values from 0 to 0.5
- feeder_price: float32 [128, 8, 96], P('scen'), may hold values from 0 to 0.5
- multiplier: float32 [128, 1024, 96], P('scen', 'bldg'), may hold values from -2 to 2
- previous_mean: float32 [128, 1024, 96], P('scen', 'bldg'), may hold values from 0 to 1
- inverse: float32 [1024, 96, 96], P('bldg'), as said below
- power_limit: float32 [1024, 96], P('bldg'), may hold values from 0.5 to 2
- weights: float32 [128], P('scen'), may hold values from 0.1 to 1
- tree_node: int32 [2, 128], P(None, 'scen'), may hold values from 0 to 15, as said below
- building_feeder: int32 [1024], P('bldg'), may hold values from 0 to 7, as said below
- feeder_limit: float32 [8, 96], replicated, may hold values from 25.6 to 128
Outputs:
- plan: float32 [128, 1024, 96], P('scen', 'bldg')
- new_multiplier: float32 [128, 1024, 96], P('scen', 'bldg')
- new_price: float32 [128, 8, 96], P('scen')
The draws below stay inside these ranges and needn't reach their ends.
Inputs may be any that keep to these rules, and one draw needn't show every extreme that they name: `tree_node`: scenarios that share a third-section node share the second-section node; each third-section node holds 8 scenarios, each second-section node 16 scenarios. `building_feeder`: every feeder has exactly 128 buildings. `inverse`: symmetric with a positive diagonal.
All inputs are finite; a program needn't handle non-finite values.
Results may differ from the reference program's by a relative error of at most 0.0001.
Values sent between devices are 32-bit elements; how exact they have to be, the bound alone decides.
A program may use at most 128 MiB of HBM per device.

```python
import math
import jax
import jax.numpy as jnp
from jax import lax

SLOTS = 96
FEED = 128
PROX = 12
S = 128
B = 1024
F = 8
N2 = 16


def draw_inverse(key, part):
    first, second = jax.random.split(key)
    diagonal = jax.random.uniform(first, (B, SLOTS), jnp.float32, 0.3, 0.6)
    noise = 0.006 * jax.random.normal(second, (B, SLOTS, SLOTS), jnp.float32)
    symmetric = 0.5 * (noise + jnp.swapaxes(noise, 1, 2))
    eye_mask = jnp.eye(SLOTS, dtype=jnp.float32)[None, :, :]
    return (symmetric * (1.0 - eye_mask) + eye_mask * diagonal[:, :, None]).astype(jnp.float32)


def draw_tree_node(key, part):
    shuffled = jax.random.permutation(key, S)
    fine_node = shuffled % (S // 8)
    coarse_node = fine_node % 8
    return jnp.stack([coarse_node, fine_node]).astype(jnp.int32)


def draw_building_feeder(key, part):
    shuffled = jax.random.permutation(key, B)
    return (shuffled // FEED).astype(jnp.int32)


def steps_of(rng, dims, shards, least, high):
    gain, own = 1.0, jax.random.fold_in(rng, 6)
    for position, parts in shards:
        draws = jnp.exp(jax.random.uniform(jax.random.fold_in(own, position), (parts,), jnp.float32, least / len(shards), high / len(shards)))
        gain = gain * jnp.repeat(draws, dims[position] // parts).reshape([-1 if axis == position else 1 for axis in range(len(dims))])
    return gain


def normal_values(own_key, dims, deviation, most, shards=(), kind=jnp.bfloat16):
    values = jax.random.normal(own_key, dims, jnp.float32) * deviation
    if len(shards) > 0:
        values = steps_of(own_key, dims, shards, -0.22, 0.18) * values
    return jnp.clip(values, min=-most, max=most).astype(kind)


def setup_inputs(seed: int = 0) -> dict:
    key_of = jax.random.split(jax.random.key(seed), 12)
    demand = normal_values(key_of[0], (S, B, SLOTS), 1.0, 6.0, ((0, 8), (1, 4)), jnp.float32)
    tariff = jnp.clip(0.5 * jax.random.uniform(key_of[1], (S, SLOTS), jnp.float32) ** steps_of(key_of[1], (S, SLOTS), ((0, 8),), -0.2, 0.2), 0.0, 0.5)
    feeder_price = jnp.clip(0.5 * jax.random.uniform(key_of[2], (S, F, SLOTS), jnp.float32) ** steps_of(key_of[2], (S, F, SLOTS), ((0, 8),), -0.2, 0.2), 0.0, 0.5)
    multiplier = normal_values(key_of[3], (S, B, SLOTS), 0.3, 2.0, ((0, 8), (1, 4)), jnp.float32)
    previous_mean = jnp.clip(1.0 * jax.random.uniform(key_of[4], (S, B, SLOTS), jnp.float32) ** steps_of(key_of[4], (S, B, SLOTS), ((0, 8), (1, 4)), -0.2, 0.2), 0.0, 1.0)
    inverse = draw_inverse(jax.random.fold_in(key_of[11], 71), 0)
    power_limit = jnp.clip(0.5 + 1.5 * jax.random.uniform(key_of[6], (B, SLOTS), jnp.float32) ** steps_of(key_of[6], (B, SLOTS), ((0, 4),), -0.2, 0.2), 0.5, 2.0)
    weights = jnp.clip(jnp.exp(math.log(1.0) - 2.3025851 * jax.random.uniform(key_of[7], (S,), jnp.float32) ** steps_of(key_of[7], (S,), ((0, 8),), -0.2, 0.2)), 0.1, 1.0)
    tree_node = draw_tree_node(jax.random.fold_in(key_of[11], 71), 0)
    building_feeder = draw_building_feeder(jax.random.fold_in(key_of[11], 71), 0)
    feeder_limit = jnp.clip(jax.random.uniform(key_of[10], (F, SLOTS), jnp.float32, 25.6, 128.0), 25.6, 128.0)
    return dict(demand=demand, tariff=tariff, feeder_price=feeder_price, multiplier=multiplier, previous_mean=previous_mean, inverse=inverse, power_limit=power_limit, weights=weights, tree_node=tree_node, building_feeder=building_feeder, feeder_limit=feeder_limit)


HIGHEST = lax.Precision.HIGHEST


def solve_prox(demand, tariff, feeder_price, multiplier, previous_mean, inverse, power_limit, building_feeder, feeders):
    member = (building_feeder[:, None] == jnp.arange(feeders)[None, :]).astype(jnp.float32)
    local_price = jnp.einsum("bf,sft->sbt", member, feeder_price, precision=HIGHEST)
    linear = tariff[:, None, :] + local_price - demand
    fixed_part = 0.5 * previous_mean - linear - multiplier
    ceiling = power_limit[None, :, :]
    iterate = jnp.clip(previous_mean, 0.0, ceiling)
    scaled_dual = jnp.zeros_like(iterate)
    for iteration in range(PROX):
        right_side = iterate - scaled_dual + fixed_part
        primal = jnp.einsum("btk,sbk->sbt", inverse, right_side, precision=HIGHEST)
        updated = jnp.clip(primal + scaled_dual, 0.0, ceiling)
        scaled_dual = scaled_dual + primal - updated
        iterate = updated
    return iterate, member


def reference(demand, tariff, feeder_price, multiplier, previous_mean, inverse, power_limit, weights, tree_node, building_feeder, feeder_limit):
    plan, member = solve_prox(demand, tariff, feeder_price, multiplier, previous_mean, inverse, power_limit, building_feeder, F)
    section_len = SLOTS // 4
    tables = [jnp.ones((1, S), jnp.float32),
              (tree_node[0][None, :] == jnp.arange(8)[:, None]).astype(jnp.float32),
              (tree_node[1][None, :] == jnp.arange(N2)[:, None]).astype(jnp.float32)]
    pieces = []
    for level in range(3):
        weighted = tables[level] * weights[None, :]
        block = plan[:, :, level * section_len:(level + 1) * section_len]
        node_total = jnp.einsum("ns,sbt->nbt", weighted, block, precision=HIGHEST)
        node_weight = jnp.sum(weighted, axis=1)
        means = node_total / node_weight[:, None, None]
        pieces.append(jnp.einsum("ns,nbt->sbt", tables[level], means, precision=HIGHEST))
    pieces.append(plan[:, :, 3 * section_len:])
    mean = jnp.concatenate(pieces, axis=2)
    new_multiplier = multiplier + 0.5 * (plan - mean)
    load = jnp.einsum("bf,sbt->sft", member, plan, precision=HIGHEST)
    new_price = jnp.maximum(0.0, feeder_price + (load - feeder_limit[None, :, :]) / FEED)
    return plan, new_multiplier, new_price
```

```python
import functools

import jax
import jax.numpy as jnp
from jax import lax
from jax.experimental import pallas as pl
from jax.experimental.pallas import tpu as pltpu
from jax.sharding import PartitionSpec as P

FEED = 128
PROX = 12
COARSE = 8
LANES = 128
MESH = pl.DeviceIdType.MESH
BF16 = jnp.bfloat16
F32 = jnp.float32


def round_up(value, unit):
    return (value + unit - 1) // unit * unit


def split3(value):
    first = value.astype(BF16)
    rest = value - first.astype(F32)
    second = rest.astype(BF16)
    third = (rest - second.astype(F32)).astype(BF16)
    return first, second, third


def share_kernel(
    pieces, demand_hbm, mult_hbm, prev_hbm, tariff_ref, price_ref, limit_ref, feeder_ref, weight_ref, tree_ref,
    keep_ref, got_ref, table_ref,
    demand, mult, prev, send, landed, table, table_landed, hot,
    load_sem, send_sem, recv_sem, table_send, table_recv,
):
    scen, slots, count = demand.shape
    half = count // 2
    each = scen // pieces
    feeders = price_ref.shape[1]
    me, column = lax.axis_index("scen"), lax.axis_index("bldg")
    core = lax.rem(me, 2)
    partner = (me + 1 - 2 * core, column)
    loads = []
    for p in range(pieces):
        rows = pl.ds(p * each, each)
        group = []
        for k, (src, dst) in enumerate(((demand_hbm, demand), (mult_hbm, mult), (prev_hbm, prev))):
            copy = pltpu.make_async_copy(src.at[rows], dst.at[rows], load_sem.at[p, k])
            copy.start()
            group.append(copy)
        loads.append(group)
    barrier = pltpu.get_barrier_semaphore()
    pl.semaphore_signal(barrier, inc=1, device_id=partner, device_id_type=MESH)

    nodes = table.shape[0]
    row = lax.broadcasted_iota(jnp.int32, (nodes, scen), 0)
    first = tree_ref[0:1, :] + 1
    second = tree_ref[1:2, :] + (1 + COARSE)
    hit = (row == 0) | (row == first) | (row == second)
    table[...] = jnp.where(hit, weight_ref[...], 0.0)
    table_ref[0] = table[...]
    one = lax.broadcasted_iota(jnp.int32, (feeders, count), 0) == feeder_ref[...]
    one = one.astype(F32).astype(BF16)
    for k in range(3):
        hot[k * feeders : (k + 1) * feeders, :] = one

    pl.semaphore_wait(barrier, 1)
    table_copy = pltpu.make_async_remote_copy(
        src_ref=table, dst_ref=table_landed, send_sem=table_send, recv_sem=table_recv,
        device_id=partner, device_id_type=MESH,
    )
    table_copy.start()

    def fill(s, offset, into):
        lanes = pl.ds(pl.multiple_of(offset, LANES), half)
        price = price_ref[s] + tariff_ref[pl.ds(s, 1), :]
        terms = jnp.concatenate(split3(price), axis=0)
        local = lax.dot_general(terms, hot[:, lanes], (((0,), (0,)), ((), ())), preferred_element_type=F32)
        before = prev[s, :, lanes]
        into[0, s] = 0.5 * before - (local - demand[s, :, lanes]) - mult[s, :, lanes]
        into[1, s] = jnp.clip(before, 0.0, limit_ref[:, lanes])

    copies = []
    for p in range(pieces):
        for copy in loads[p]:
            copy.wait()
        for s in range(p * each, (p + 1) * each):
            fill(s, half - core * half, send)
        rows = pl.ds(p * each, each)
        copy = pltpu.make_async_remote_copy(
            src_ref=send.at[:, rows], dst_ref=landed.at[:, rows],
            send_sem=send_sem.at[p], recv_sem=recv_sem.at[p],
            device_id=partner, device_id_type=MESH,
        )
        copy.start()
        copies.append(copy)
    for s in range(scen):
        fill(s, core * half, keep_ref)
    table_copy.wait()
    table_ref[1] = table_landed[...]
    for p in range(pieces):
        copies[p].wait_recv()
        rows = pl.ds(p * each, each)
        got_ref[:, rows] = landed[:, rows]
    for copy in copies:
        copy.wait_send()


def share(demand, mult, prev, tariff, price, limit, feeder, weights, tree, nodes):
    scen, slots, count = demand.shape
    feeders = price.shape[1]
    half = count // 2
    pieces = 4
    vmem = pl.BlockSpec(memory_space=pltpu.VMEM)
    hbm = pl.BlockSpec(memory_space=pl.ANY)
    dma = pltpu.SemaphoreType.DMA
    pair = (2, scen, slots, half)
    return pl.pallas_call(
        functools.partial(share_kernel, pieces),
        in_specs=[hbm, hbm, hbm] + [vmem] * 6,
        out_specs=[vmem, vmem, vmem],
        out_shape=[
            jax.ShapeDtypeStruct(pair, F32),
            jax.ShapeDtypeStruct(pair, F32),
            jax.ShapeDtypeStruct((2, nodes, scen), F32),
        ],
        scratch_shapes=[
            pltpu.VMEM(demand.shape, F32), pltpu.VMEM(demand.shape, F32), pltpu.VMEM(demand.shape, F32),
            pltpu.VMEM(pair, F32), pltpu.VMEM(pair, F32),
            pltpu.VMEM((nodes, scen), F32), pltpu.VMEM((nodes, scen), F32),
            pltpu.VMEM((3 * feeders, count), BF16),
            dma((pieces, 3)), dma((pieces,)), dma((pieces,)), dma(()), dma(()),
        ],
        compiler_params=pltpu.CompilerParams(
            collective_id=1, has_side_effects=True, vmem_limit_bytes=40 * 2**20
        ),
        name="share",
    )(demand, mult, prev, tariff, price, limit, feeder, weights, tree)


def prox_kernel(
    nodes, pieces, inv_hbm, limit_ref, feeder_ref, keep_ref, got_ref, table_ref,
    mine_ref, theirs_ref, sums_ref, load_ref,
    inv, w_ref, fixed_ref, z_ref, u_ref, both_ref, cap_ref, inv_sem,
):
    slots, _, half = inv.shape
    _, scen, _, _ = keep_ref.shape
    wide = 2 * scen
    feeders = load_ref.shape[1]
    core = lax.rem(lax.axis_index("scen"), 2)
    lanes = pl.ds(pl.multiple_of(core * half, LANES), half)
    each = slots // pieces

    def inv_copy(p):
        rows = pl.ds(p * each, each)
        return pltpu.make_async_copy(inv_hbm.at[rows, :, lanes], inv.at[rows], inv_sem.at[p])

    for p in range(pieces):
        inv_copy(p).start()
    cap_ref[...] = jnp.transpose(limit_ref[:, lanes], (1, 0))

    for k, source in enumerate((keep_ref, got_ref)):
        part = slice(k * scen, (k + 1) * scen)
        fixed = jnp.transpose(source[0], (2, 0, 1))
        start = jnp.transpose(source[1], (2, 0, 1))
        right = start + fixed
        high = right.astype(BF16)
        fixed_ref[:, part, :] = fixed
        both_ref[:, part, :] = high
        both_ref[:, wide + k * scen : wide + (k + 1) * scen, :] = (right - high.astype(F32)).astype(BF16)
    u_ref[...] = jnp.zeros_like(u_ref)

    for p in range(pieces):
        inv_copy(p).wait()
        rows = slice(p * each, (p + 1) * each)
        full = jnp.transpose(inv[rows], (2, 0, 1))
        high = full.astype(BF16)
        w_ref[:, rows, :slots] = high
        w_ref[:, rows, LANES : LANES + slots] = (full - high.astype(F32)).astype(BF16)

    def iteration(i, carry):
        for b in range(half):
            out = jnp.dot(both_ref[b], w_ref[b], preferred_element_type=F32)
            primal = out[:wide, :slots] + (out[:wide, LANES : LANES + slots] + out[wide:, :slots])
            moved = primal + u_ref[b]
            fresh = jnp.clip(moved, 0.0, cap_ref[b : b + 1, :])
            dual = moved - fresh
            right = fresh - dual + fixed_ref[b]
            high = right.astype(BF16)
            z_ref[b] = fresh
            u_ref[b] = dual
            both_ref[b, :wide] = high
            both_ref[b, wide:] = (right - high.astype(F32)).astype(BF16)
        return carry

    lax.fori_loop(0, PROX, iteration, 0)

    mine_ref[...] = jnp.transpose(z_ref[:, :scen, :], (1, 2, 0))
    theirs_ref[...] = jnp.transpose(z_ref[:, scen:, :], (1, 2, 0))

    length = slots // 4
    tail = nodes * length
    rest = sums_ref.shape[0] - tail
    sums_ref[pl.ds(tail, rest), :] = jnp.zeros((rest, half), F32)
    plans = (mine_ref, theirs_ref)

    def add_nodes(level, at_once):
        part = slice(level * length, (level + 1) * length)

        def body(step, base):
            first = base + step * at_once
            totals = [0.0] * at_once
            accs = [jnp.zeros((length, half), F32)] * at_once
            for k in range(2):
                for s in range(scen):
                    block = plans[k][s, part, :]
                    for j in range(at_once):
                        factor = table_ref[k, first + j, s]
                        totals[j] = totals[j] + factor
                        accs[j] = accs[j] + factor * block
            for j in range(at_once):
                sums_ref[pl.ds(pl.multiple_of((first + j) * length, 8), length), :] = accs[j]
                sums_ref[pl.ds(tail + first + j, 1), :] = jnp.full((1, half), totals[j], F32)
            return base

        return body

    add_nodes(0, 1)(0, 0)
    lax.fori_loop(0, COARSE // 4, add_nodes(1, 4), 1)
    lax.fori_loop(0, (nodes - 1 - COARSE) // 4, add_nodes(2, 4), 1 + COARSE)

    one = lax.broadcasted_iota(jnp.int32, (feeders, half), 0) == feeder_ref[:, lanes]
    one = one.astype(F32).astype(BF16)
    for k in range(2):
        for s in range(scen):
            value = plans[k][s]
            high = value.astype(BF16)
            low = (value - high.astype(F32)).astype(BF16)
            dims = (((1,), (1,)), ((), ()))
            load_ref[k * scen + s] = lax.dot_general(
                one, high, dims, preferred_element_type=F32
            ) + lax.dot_general(one, low, dims, preferred_element_type=F32)


def prox(inverse, limit, feeder, keep, got, table, nodes, feeders, rows):
    slots, _, count = inverse.shape
    _, scen, _, half = keep.shape
    pieces = slots // 16
    vmem = pl.BlockSpec(memory_space=pltpu.VMEM)
    plan = jax.ShapeDtypeStruct((scen, slots, half), F32)
    state = pltpu.VMEM((half, 2 * scen, slots), F32)
    return pl.pallas_call(
        functools.partial(prox_kernel, nodes, pieces),
        in_specs=[
            pl.BlockSpec(memory_space=pl.ANY), vmem, vmem, vmem, vmem,
            pl.BlockSpec(memory_space=pltpu.SMEM),
        ],
        out_specs=[vmem] * 4,
        out_shape=[
            plan, plan,
            jax.ShapeDtypeStruct((rows, half), F32),
            jax.ShapeDtypeStruct((2 * scen, feeders, slots), F32),
        ],
        scratch_shapes=[
            pltpu.VMEM((slots, slots, half), F32),
            pltpu.VMEM((half, slots, 2 * LANES), BF16),
            state, state, state,
            pltpu.VMEM((half, 4 * scen, slots), BF16),
            pltpu.VMEM((half, slots), F32),
            pltpu.SemaphoreType.DMA((pieces,)),
        ],
        compiler_params=pltpu.CompilerParams(vmem_limit_bytes=50 * 2**20),
        name="prox",
    )(inverse, limit, feeder, keep, got, table)


def exchange_kernel(
    scen_size, bldg_size, sums_ref, theirs_ref, load_ref,
    full_ref, back_ref, total_ref,
    landed, own, whole, other, plan_landed, load_first, load_mine, load_landed,
    rs_send, rs_recv, ag_send, ag_recv, on_send, on_recv, plan_send, plan_recv, pair_send, pair_recv, load_send, load_recv,
):
    chips = scen_size // 2
    me, column = lax.axis_index("scen"), lax.axis_index("bldg")
    core = lax.rem(me, 2)
    chip = lax.div(me, 2)
    chunk, half = own.shape
    scen = total_ref.shape[0]
    partner = (me + 1 - 2 * core, column)
    peers = [(lax.rem(me + 2 * k, scen_size), column) for k in range(1, chips)]
    beside = [(me, lax.rem(column + k, bldg_size)) for k in range(1, bldg_size)]
    barrier = pltpu.get_barrier_semaphore()
    for peer in [partner] + peers + beside:
        pl.semaphore_signal(barrier, inc=1, device_id=peer, device_id_type=MESH)
    pl.semaphore_wait(barrier, chips + bldg_size - 1)

    def rows_of(index):
        return pl.ds(pl.multiple_of(index * chunk, 8), chunk)

    def remote(src, dst, send_sem, recv_sem, device):
        copy = pltpu.make_async_remote_copy(
            src_ref=src, dst_ref=dst, send_sem=send_sem, recv_sem=recv_sem,
            device_id=device, device_id_type=MESH,
        )
        copy.start()
        return copy

    scatter = [
        remote(sums_ref.at[rows_of(lax.div(peer[0], 2))], landed.at[k], rs_send.at[k], rs_recv.at[k], peer)
        for k, peer in enumerate(peers)
    ]
    pair_load = remote(load_ref.at[pl.ds(scen, scen)], load_first, pair_send, pair_recv, partner)
    plan_copy = remote(theirs_ref, plan_landed, plan_send, plan_recv, partner)

    pair_load.wait_recv()
    load_mine[...] = load_ref[pl.ds(0, scen)] + load_first[...]
    loads = [
        remote(load_mine, load_landed.at[k], load_send.at[k], load_recv.at[k], peer)
        for k, peer in enumerate(beside)
    ]

    for copy in scatter:
        copy.wait_recv()
    acc = sums_ref[rows_of(chip), :]
    for k in range(chips - 1):
        acc = acc + landed[k]
    own[...] = acc
    gather = [
        remote(own, whole.at[k + 1], ag_send.at[k], ag_recv.at[k], peer)
        for k, peer in enumerate(peers)
    ]
    onward = [remote(own, other.at[0], on_send.at[0], on_recv.at[0], partner)]
    lanes = pl.ds(pl.multiple_of(core * half, LANES), half)
    full_ref[rows_of(chip), lanes] = acc

    total = load_mine[...]
    for k, copy in enumerate(loads):
        copy.wait_recv()
        total = total + load_landed[k]
    total_ref[...] = total
    plan_copy.wait_recv()
    back_ref[...] = plan_landed[...]

    for k in range(1, chips):
        gather[k - 1].wait_recv()
        onward.append(remote(whole.at[k], other.at[k], on_send.at[k], on_recv.at[k], partner))
        source = lax.rem(chip - k + chips, chips)
        full_ref[rows_of(source), lanes] = whole[k]
    away = pl.ds(pl.multiple_of(half - core * half, LANES), half)
    for k in range(chips):
        onward[k].wait_recv()
        source = lax.rem(chip - k + chips, chips)
        full_ref[rows_of(source), away] = other[k]
    for copy in scatter + [pair_load, plan_copy] + loads + gather + onward:
        copy.wait_send()


def exchange(sums, theirs, load):
    scen_size, bldg_size = lax.axis_size("scen"), lax.axis_size("bldg")
    chips = scen_size // 2
    rows, half = sums.shape
    chunk = rows // chips
    dma = pltpu.SemaphoreType.DMA
    vmem = pl.BlockSpec(memory_space=pltpu.VMEM)
    mine = (load.shape[0] // 2,) + load.shape[1:]
    return pl.pallas_call(
        functools.partial(exchange_kernel, scen_size, bldg_size),
        in_specs=[vmem] * 3,
        out_specs=[vmem] * 3,
        out_shape=[
            jax.ShapeDtypeStruct((rows, 2 * half), F32),
            jax.ShapeDtypeStruct(theirs.shape, F32),
            jax.ShapeDtypeStruct(mine, F32),
        ],
        scratch_shapes=[
            pltpu.VMEM((chips - 1, chunk, half), F32),
            pltpu.VMEM((chunk, half), F32),
            pltpu.VMEM((chips, chunk, half), F32),
            pltpu.VMEM((chips, chunk, half), F32),
            pltpu.VMEM(theirs.shape, F32),
            pltpu.VMEM(mine, F32),
            pltpu.VMEM(mine, F32),
            pltpu.VMEM((bldg_size - 1,) + mine, F32),
            dma((chips - 1,)), dma((chips - 1,)),
            dma((chips - 1,)), dma((chips - 1,)),
            dma((chips,)), dma((chips,)),
            dma(()), dma(()), dma(()), dma(()),
            dma((bldg_size - 1,)), dma((bldg_size - 1,)),
        ],
        compiler_params=pltpu.CompilerParams(
            collective_id=0, has_side_effects=True, vmem_limit_bytes=24 * 2**20
        ),
        name="exchange",
    )(sums, theirs, load)


def spread_kernel(
    nodes, tree_ref, full_ref, mine_ref, back_ref, mult_ref, price_ref, load_ref, limit_ref,
    plan_ref, out_ref, new_price_ref, mean_ref,
):
    step = pl.program_id(0)
    each, slots, count = mult_ref.shape
    half = count // 2
    length = slots // 4
    tail = nodes * length
    core = lax.rem(lax.axis_index("scen"), 2)

    @pl.when(step == 0)
    def _():
        def divide(n, carry):
            share = full_ref[pl.ds(pl.multiple_of(n * length, 8), length), :]
            mean_ref[n] = share / full_ref[pl.ds(tail + n, 1), :]
            return carry

        lax.fori_loop(0, nodes, divide, 0)

    for j in range(each):
        s = step * each + j
        places = (0, tree_ref[0, s] + 1, tree_ref[1, s] + (1 + COARSE))
        for source, offset in ((mine_ref, core * half), (back_ref, half - core * half)):
            lanes = pl.ds(pl.multiple_of(offset, LANES), half)
            plan_ref[j, :, lanes] = source[j]
            for level in range(4):
                part = slice(level * length, (level + 1) * length)
                plan = source[j, part, :]
                mean = plan if level == 3 else mean_ref[places[level], :, lanes]
                out_ref[j, part, lanes] = mult_ref[j, part, lanes] + 0.5 * (plan - mean)
    new_price_ref[...] = jnp.maximum(0.0, price_ref[...] + (load_ref[...] - limit_ref[...][None]) / FEED)


def spread(tree, full, mine, back, mult, price, load, limit, nodes):
    scen, slots, count = mult.shape
    feeders = price.shape[1]
    each = 4
    block = lambda *shape: pl.BlockSpec((each,) + shape, lambda i: (i, 0, 0))
    return pl.pallas_call(
        functools.partial(spread_kernel, nodes),
        grid=(scen // each,),
        in_specs=[
            pl.BlockSpec(memory_space=pltpu.SMEM),
            pl.BlockSpec(full.shape, lambda i: (0, 0)),
            block(slots, count // 2), block(slots, count // 2), block(slots, count),
            block(feeders, slots), block(feeders, slots),
            pl.BlockSpec(limit.shape, lambda i: (0, 0)),
        ],
        out_specs=[block(slots, count), block(slots, count), block(feeders, slots)],
        out_shape=[
            jax.ShapeDtypeStruct(mult.shape, F32),
            jax.ShapeDtypeStruct(mult.shape, F32),
            jax.ShapeDtypeStruct(price.shape, F32),
        ],
        scratch_shapes=[pltpu.VMEM((nodes, slots // 4, count), F32)],
        compiler_params=pltpu.CompilerParams(vmem_limit_bytes=24 * 2**20),
        name="spread",
    )(tree, full, mine, back, mult, price, load, limit)


def per_device(
    demand,
    tariff,
    feeder_price,
    multiplier,
    previous_mean,
    inverse,
    power_limit,
    weights,
    tree_node,
    building_feeder,
    feeder_limit,
):
    scen_size = lax.axis_size("scen")
    scen, count, slots = demand.shape
    feeders = feeder_price.shape[1]
    nodes = 1 + COARSE + scen_size * scen // 8
    rows = round_up(nodes * (slots // 4) + nodes, 8 * (scen_size // 2))

    def turned(value):
        return jnp.transpose(value, (0, 2, 1))

    limit = jnp.transpose(power_limit, (1, 0))
    feeder = building_feeder.reshape(1, count)
    mult = turned(multiplier)
    keep, got, table = share(
        turned(demand), mult, turned(previous_mean), tariff, feeder_price, limit, feeder,
        weights.reshape(1, scen), tree_node, nodes,
    )
    mine, theirs, sums, load = prox(
        jnp.transpose(inverse, (1, 2, 0)), limit, feeder, keep, got, table, nodes, feeders, rows
    )
    full, back, total = exchange(sums, theirs, load)
    plan, new_multiplier, new_price = spread(
        tree_node, full, mine, back, mult, feeder_price, total, feeder_limit, nodes
    )
    return turned(plan), turned(new_multiplier), new_price


def solution(mesh):
    in_specs = (
        P("scen", "bldg", None),
        P("scen", None),
        P("scen", None, None),
        P("scen", "bldg", None),
        P("scen", "bldg", None),
        P("bldg", None, None),
        P("bldg", None),
        P("scen"),
        P(None, "scen"),
        P("bldg"),
        P(),
    )
    out_specs = (P("scen", "bldg", None), P("scen", "bldg", None), P("scen", None, None))
    return jax.shard_map(
        per_device, mesh=mesh, in_specs=in_specs, out_specs=out_specs, check_vma=False
    )
```

```python
import functools

import jax
import jax.numpy as jnp
from jax import lax
from jax.experimental import pallas as pl
from jax.experimental.pallas import tpu as pltpu
from jax.sharding import PartitionSpec as P

FEED = 128
PROX = 12
COARSE = 8
LANES = 128
MESH = pl.DeviceIdType.MESH
BF16 = jnp.bfloat16
F32 = jnp.float32


def round_up(value, unit):
    return (value + unit - 1) // unit * unit


def split3(value):
    first = value.astype(BF16)
    rest = value - first.astype(F32)
    second = rest.astype(BF16)
    third = (rest - second.astype(F32)).astype(BF16)
    return first, second, third


def solve_kernel(
    nodes, scen_size, bldg_size,
    demand_hbm, mult_hbm, prev_hbm, inv_hbm, tariff_hbm, price_hbm, limit_hbm, feeder_hbm, weight_hbm, tree_hbm,
    mine_ref, back_ref, full_ref, total_ref,
    demand, mult, prev, inv, tariff, price, limit, feeder, weight, tree,
    send, landed, keep, table, table_landed, hot, factor, cap, w_ref, fixed_ref, z_ref, u_ref, both_ref,
    packed, sums, sums_landed, theirs, load, load_first, load_mine, load_landed,
    in_sem, inv_sem, small_sem, send_sem, recv_sem, table_send, table_recv,
    rs_send, rs_recv, ag_send, ag_recv, on_send, on_recv,
    plan_send, plan_recv, pair_send, pair_recv, load_send, load_recv,
):
    scen, slots, count = demand.shape
    half = count // 2
    wide = 2 * scen
    groups, group_rows = sums.shape[:2]
    size = half // groups
    feeders = total_ref.shape[1]
    pieces = in_sem.shape[0]
    each = scen // pieces
    inv_pieces = inv_sem.shape[0]
    inv_each = slots // inv_pieces
    length = slots // 4
    chips = scen_size // 2
    chunk = group_rows // chips
    me, column = lax.axis_index("scen"), lax.axis_index("bldg")
    core = lax.rem(me, 2)
    chip = lax.div(me, 2)
    partner = (me + 1 - 2 * core, column)
    peers = [(lax.rem(me + 2 * k, scen_size), column) for k in range(1, chips)]
    beside = [(me, lax.rem(column + k, bldg_size)) for k in range(1, bldg_size)]
    own_lanes = pl.ds(pl.multiple_of(core * half, LANES), half)
    away_lanes = pl.ds(pl.multiple_of(half - core * half, LANES), half)

    def remote(src, dst, send, recv, device):
        copy = pltpu.make_async_remote_copy(
            src_ref=src, dst_ref=dst, send_sem=send, recv_sem=recv, device_id=device, device_id_type=MESH
        )
        copy.start()
        return copy

    def local(src, dst, sem):
        copy = pltpu.make_async_copy(src, dst, sem)
        copy.start()
        return copy

    barrier = pltpu.get_barrier_semaphore()
    for peer in [partner] + peers + beside:
        pl.semaphore_signal(barrier, inc=1, device_id=peer, device_id_type=MESH)
    small = [
        local(src, dst, small_sem.at[k])
        for k, (src, dst) in enumerate((
            (tariff_hbm, tariff), (price_hbm, price), (limit_hbm, limit),
            (feeder_hbm, feeder), (weight_hbm, weight), (tree_hbm, tree),
        ))
    ]
    loads = []
    for p in range(pieces):
        rows = pl.ds(p * each, each)
        loads.append([
            local(src.at[rows], dst.at[rows], in_sem.at[p, k])
            for k, (src, dst) in enumerate(((prev_hbm, prev), (demand_hbm, demand), (mult_hbm, mult)))
        ])
    inv_loads = []
    for p in range(inv_pieces):
        rows = pl.ds(p * inv_each, inv_each)
        inv_loads.append(local(inv_hbm.at[rows, :, own_lanes], inv.at[rows], inv_sem.at[p]))

    for copy in small:
        copy.wait()
    padded = table.shape[0]
    row = lax.broadcasted_iota(jnp.int32, (padded, scen), 0)
    hit = (row == 0) | (row == tree[0:1, :] + 1) | (row == tree[1:2, :] + (1 + COARSE))
    table[...] = jnp.where(hit, weight[...], 0.0)
    one = lax.broadcasted_iota(jnp.int32, (feeders, count), 0) == feeder[...]
    one = one.astype(F32).astype(BF16)
    for k in range(3):
        hot[k * feeders : (k + 1) * feeders, :] = one
    pl.semaphore_wait(barrier, chips + bldg_size - 1)
    table_copy = remote(table, table_landed, table_send, table_recv, partner)

    def fill(s, lanes, into):
        terms = jnp.concatenate(split3(price[s] + tariff[pl.ds(s, 1), :]), axis=0)
        paid = lax.dot_general(terms, hot[:, lanes], (((0,), (0,)), ((), ())), preferred_element_type=F32)
        before = prev[s, :, lanes]
        into[0, s] = 0.5 * before - (paid - demand[s, :, lanes]) - mult[s, :, lanes]
        into[1, s] = jnp.clip(before, 0.0, limit[:, lanes])

    swaps = []
    for p in range(pieces):
        for copy in loads[p]:
            copy.wait()
        for s in range(p * each, (p + 1) * each):
            fill(s, away_lanes, send)
        rows = pl.ds(p * each, each)
        swaps.append(remote(send.at[:, rows], landed.at[:, rows], send_sem.at[p], recv_sem.at[p], partner))
    for s in range(scen):
        fill(s, own_lanes, keep)

    def begin(k, source):
        fixed = jnp.transpose(source[0], (2, 0, 1))
        right = jnp.transpose(source[1], (2, 0, 1)) + fixed
        high = right.astype(BF16)
        fixed_ref[:, k * scen : (k + 1) * scen, :] = fixed
        both_ref[:, k * scen : (k + 1) * scen, :] = high
        both_ref[:, wide + k * scen : wide + (k + 1) * scen, :] = (right - high.astype(F32)).astype(BF16)

    begin(0, keep)
    cap[...] = jnp.transpose(limit[:, own_lanes], (1, 0))
    u_ref[...] = jnp.zeros_like(u_ref)
    for p in range(inv_pieces):
        inv_loads[p].wait()
        rows = slice(p * inv_each, (p + 1) * inv_each)
        exact = jnp.transpose(inv[rows], (2, 0, 1))
        high = exact.astype(BF16)
        w_ref[:, rows, :slots] = high
        w_ref[:, rows, LANES : LANES + slots] = (exact - high.astype(F32)).astype(BF16)
    table_copy.wait()
    lane = lax.broadcasted_iota(jnp.int32, (padded, LANES), 1)
    for s in range(scen):
        factor[s] = jnp.where(lane < size, table[:, s : s + 1], table_landed[:, s : s + 1])
    for copy in swaps:
        copy.wait_recv()
    begin(1, landed)

    def step(b):
        out = jnp.dot(both_ref[b], w_ref[b], preferred_element_type=F32)
        primal = out[:wide, :slots] + (out[:wide, LANES : LANES + slots] + out[wide:, :slots])
        moved = primal + u_ref[b]
        fresh = jnp.clip(moved, 0.0, cap[b : b + 1, :])
        dual = moved - fresh
        right = fresh - dual + fixed_ref[b]
        high = right.astype(BF16)
        z_ref[b] = fresh
        u_ref[b] = dual
        both_ref[b, :wide] = high
        both_ref[b, wide:] = (right - high.astype(F32)).astype(BF16)

    low_lanes = lax.broadcasted_iota(jnp.int32, (length, LANES), 1) < size
    tail = (nodes + 1) // 2 * length

    def add_up(g):
        part = slice(g * size, (g + 1) * size)
        packed[...] = jnp.concatenate(
            [
                jnp.transpose(z_ref[part, :scen, :], (1, 0, 2)),
                jnp.transpose(z_ref[part, scen:, :], (1, 0, 2)),
            ],
            axis=1,
        ).swapaxes(1, 2)[:, : 3 * length, :]
        whole = []
        for n in range(nodes):
            level = 0 if n == 0 else (1 if n <= COARSE else 2)
            acc = jnp.zeros((length, LANES), F32)
            for s in range(scen):
                acc = acc + factor[s, n : n + 1, :] * packed[s, level * length : (level + 1) * length, :]
            whole.append(acc + pltpu.roll(acc, size, 1))
            if n % 2 == 1 or n == nodes - 1:
                both = jnp.where(low_lanes, whole[n - n % 2], whole[n])
                sums[g, n // 2 * length : (n // 2 + 1) * length, :] = both
        rest = group_rows - tail
        counted = jnp.sum(table[...] + table_landed[...], axis=1, keepdims=True)
        sums[g, tail : tail + padded, :] = jnp.broadcast_to(counted, (padded, LANES))
        if rest > padded:
            sums[g, tail + padded :, :] = jnp.zeros((rest - padded, LANES), F32)

    def rows_of(index):
        return pl.ds(pl.multiple_of(index * chunk, 8), chunk)

    def scatter(g):
        return [
            remote(
                sums.at[g, rows_of(lax.div(peer[0], 2))], sums_landed.at[g, k],
                rs_send.at[g, k], rs_recv.at[g, k], peer,
            )
            for k, peer in enumerate(peers)
        ]

    def gather(g, scattered):
        for copy in scattered:
            copy.wait_recv()
        acc = sums[g, rows_of(chip), :]
        for k in range(chips - 1):
            acc = acc + sums_landed[g, k]
        full_ref[core, g, rows_of(chip), :] = acc
        spot = full_ref.at[core, g, rows_of(chip)]
        copies = [remote(spot, spot, ag_send.at[g, k], ag_recv.at[g, k], peer) for k, peer in enumerate(peers)]
        return copies, [remote(spot, spot, on_send.at[g, 0], on_recv.at[g, 0], partner)]

    def onward(g, gathered, passed):
        for k in range(1, chips):
            gathered[k - 1].wait_recv()
            spot = full_ref.at[core, g, rows_of(lax.rem(chip - k + chips, chips))]
            passed.append(remote(spot, spot, on_send.at[g, k], on_recv.at[g, k], partner))

    def solve(g, low, high):
        def twice(i, carry):
            for _ in range(2):
                for b in range(g * size, (g + 1) * size):
                    step(b)
            return carry

        lax.fori_loop(low, high, twice, 0)

    pending = []
    turns = PROX // 2
    done = []
    for g in range(groups):
        if g == 0:
            solve(g, 0, turns)
        else:
            solve(g, 0, turns // 3)
            gathered, passed = gather(g - 1, scattered)
            solve(g, turns // 3, 2 * turns // 3)
            onward(g - 1, gathered, passed)
            solve(g, 2 * turns // 3, turns)
            pending += scattered + gathered
            done += passed
        add_up(g)
        scattered = scatter(g)

    theirs[...] = jnp.transpose(z_ref[:, scen:, :], (1, 2, 0))
    plan_copy = remote(theirs, back_ref, plan_send, plan_recv, partner)
    mine_ref[...] = jnp.transpose(z_ref[:, :scen, :], (1, 2, 0))

    def loads_of(source):
        dims = (((1,), (1,)), ((), ()))
        one = hot[:feeders, own_lanes]
        for s in range(scen):
            value = source[s]
            high = value.astype(BF16)
            low = (value - high.astype(F32)).astype(BF16)
            yield s, lax.dot_general(one, high, dims, preferred_element_type=F32) + lax.dot_general(
                one, low, dims, preferred_element_type=F32
            )

    for s, value in loads_of(theirs):
        load[s] = value
    pair_load = remote(load, load_first, pair_send, pair_recv, partner)
    for s, value in loads_of(mine_ref):
        load_mine[s] = value
    last = groups - 1
    gathered, passed = gather(last, scattered)
    pair_load.wait_recv()
    load_mine[...] = load_mine[...] + load_first[...]
    spread_loads = [
        remote(load_mine, load_landed.at[k], load_send.at[k], load_recv.at[k], peer)
        for k, peer in enumerate(beside)
    ]
    onward(last, gathered, passed)
    total = load_mine[...]
    for k, copy in enumerate(spread_loads):
        copy.wait_recv()
        total = total + load_landed[k]
    total_ref[...] = total
    plan_copy.wait_recv()
    for copy in done + passed:
        copy.wait_recv()
    for copy in swaps + pending + scattered + gathered + done + passed + spread_loads + [plan_copy, pair_load]:
        copy.wait_send()


def solve(demand, mult, prev, inverse, tariff, price, limit, feeder, weights, tree, nodes, groups, rows):
    scen_size, bldg_size = lax.axis_size("scen"), lax.axis_size("bldg")
    chips = scen_size // 2
    scen, slots, count = demand.shape
    feeders = price.shape[1]
    half = count // 2
    length = slots // 4
    padded = round_up(nodes, 8)
    chunk = rows // chips
    vmem = pl.BlockSpec(memory_space=pltpu.VMEM)
    hbm = pl.BlockSpec(memory_space=pltpu.HBM)
    dma = pltpu.SemaphoreType.DMA
    big = pltpu.VMEM(demand.shape, F32)
    pair = pltpu.VMEM((2, scen, slots, half), F32)
    state = pltpu.VMEM((half, 2 * scen, slots), F32)
    held = lambda array: pltpu.VMEM(array.shape, array.dtype)
    loads = pltpu.VMEM((scen, feeders, slots), F32)
    return pl.pallas_call(
        functools.partial(solve_kernel, nodes, scen_size, bldg_size),
        in_specs=[hbm] * 10,
        out_specs=[vmem] * 4,
        out_shape=[
            jax.ShapeDtypeStruct((scen, slots, half), F32),
            jax.ShapeDtypeStruct((scen, slots, half), F32),
            jax.ShapeDtypeStruct((2, groups, rows, half), F32),
            jax.ShapeDtypeStruct((scen, feeders, slots), F32),
        ],
        scratch_shapes=[
            big, big, big,
            pltpu.VMEM((slots, slots, half), F32),
            held(tariff), held(price), held(limit), held(feeder), held(weights), held(tree),
            pair, pair, pair,
            pltpu.VMEM((padded, scen), F32), pltpu.VMEM((padded, scen), F32),
            pltpu.VMEM((3 * feeders, count), BF16),
            pltpu.VMEM((scen, padded, LANES), F32),
            pltpu.VMEM((half, slots), F32),
            pltpu.VMEM((half, slots, 2 * LANES), BF16),
            state, state, state,
            pltpu.VMEM((half, 4 * scen, slots), BF16),
            pltpu.VMEM((scen, 3 * length, LANES), F32),
            pltpu.VMEM((groups, rows, LANES), F32),
            pltpu.VMEM((groups, chips - 1, chunk, LANES), F32),
            pltpu.VMEM((scen, slots, half), F32),
            loads, loads, loads,
            pltpu.VMEM((bldg_size - 1, scen, feeders, slots), F32),
            dma((4, 3)), dma((slots // 16,)), dma((6,)), dma((4,)), dma((4,)), dma(()), dma(()),
            dma((groups, chips - 1)), dma((groups, chips - 1)),
            dma((groups, chips - 1)), dma((groups, chips - 1)),
            dma((groups, chips)), dma((groups, chips)),
            dma(()), dma(()), dma(()), dma(()),
            dma((bldg_size - 1,)), dma((bldg_size - 1,)),
        ],
        compiler_params=pltpu.CompilerParams(
            collective_id=0, has_side_effects=True, vmem_limit_bytes=42 * 2**20
        ),
        name="solve",
    )(*(pltpu.with_memory_space_constraint(x, pltpu.HBM) for x in (
        demand, mult, prev, inverse, tariff, price, limit, feeder, weights, tree)))


def spread_kernel(
    nodes, tree_ref, full_ref, mine_ref, back_ref, mult_ref, price_ref, load_ref, limit_ref,
    plan_ref, out_ref, new_price_ref, mean_ref,
):
    step = pl.program_id(0)
    each, slots, count = mult_ref.shape
    half = count // 2
    length = slots // 4
    tail = (nodes + 1) // 2 * length
    groups = full_ref.shape[1]
    size = half // groups
    core = lax.rem(lax.axis_index("scen"), 2)

    @pl.when(step == 0)
    def _():
        low_lanes = lax.broadcasted_iota(jnp.int32, (length, half), 1) < size
        for c in range(2):
            for n in range(nodes):
                count_row = full_ref[c, 0, tail + n : tail + n + 1, :]
                block = slice(n // 2 * length, (n // 2 + 1) * length)
                first = full_ref[c, 0, block, :]
                second = full_ref[c, 1, block, :]
                if n % 2 == 0:
                    share = jnp.where(low_lanes, first, pltpu.roll(second, size, 1))
                else:
                    share = jnp.where(low_lanes, pltpu.roll(first, size, 1), second)
                mean_ref[n, :, c * half : (c + 1) * half] = share / count_row

    for j in range(each):
        s = step * each + j
        places = (0, tree_ref[0, s] + 1, tree_ref[1, s] + (1 + COARSE))
        for source, offset in ((mine_ref, core * half), (back_ref, half - core * half)):
            lanes = pl.ds(pl.multiple_of(offset, LANES), half)
            plan_ref[j, :, lanes] = source[j]
            for level in range(4):
                part = slice(level * length, (level + 1) * length)
                plan = source[j, part, :]
                mean = plan if level == 3 else mean_ref[places[level], :, lanes]
                out_ref[j, part, lanes] = mult_ref[j, part, lanes] + 0.5 * (plan - mean)
    new_price_ref[...] = jnp.maximum(0.0, price_ref[...] + (load_ref[...] - limit_ref[...][None]) / FEED)


def spread(tree, full, mine, back, mult, price, load, limit, nodes):
    scen, slots, count = mult.shape
    feeders = price.shape[1]
    each = 4
    block = lambda *shape: pl.BlockSpec((each,) + shape, lambda i: (i, 0, 0))
    return pl.pallas_call(
        functools.partial(spread_kernel, nodes),
        grid=(scen // each,),
        in_specs=[
            pl.BlockSpec(memory_space=pltpu.SMEM),
            pl.BlockSpec(full.shape, lambda i: (0, 0, 0, 0)),
            block(slots, count // 2), block(slots, count // 2), block(slots, count),
            block(feeders, slots), block(feeders, slots),
            pl.BlockSpec(limit.shape, lambda i: (0, 0)),
        ],
        out_specs=[block(slots, count), block(slots, count), block(feeders, slots)],
        out_shape=[
            jax.ShapeDtypeStruct(mult.shape, F32),
            jax.ShapeDtypeStruct(mult.shape, F32),
            jax.ShapeDtypeStruct(price.shape, F32),
        ],
        scratch_shapes=[pltpu.VMEM((nodes, slots // 4, count), F32)],
        compiler_params=pltpu.CompilerParams(vmem_limit_bytes=24 * 2**20),
        name="spread",
    )(tree, full, mine, back, mult, price, load, limit)


def per_device(
    demand,
    tariff,
    feeder_price,
    multiplier,
    previous_mean,
    inverse,
    power_limit,
    weights,
    tree_node,
    building_feeder,
    feeder_limit,
):
    scen_size = lax.axis_size("scen")
    scen, count, slots = demand.shape
    nodes = 1 + COARSE + scen_size * scen // 8
    groups = 2
    rows = round_up((nodes + 1) // 2 * (slots // 4) + round_up(nodes, 8), 8 * (scen_size // 2))

    def turned(value):
        return jnp.transpose(value, (0, 2, 1))

    limit = jnp.transpose(power_limit, (1, 0))
    mult = turned(multiplier)
    mine, back, full, total = solve(
        turned(demand), mult, turned(previous_mean), jnp.transpose(inverse, (1, 2, 0)), tariff, feeder_price,
        limit, building_feeder.reshape(1, count), weights.reshape(1, scen), tree_node, nodes, groups, rows,
    )
    plan, new_multiplier, new_price = spread(
        tree_node, full, mine, back, mult, feeder_price, total, feeder_limit, nodes
    )
    return turned(plan), turned(new_multiplier), new_price


def solution(mesh):
    in_specs = (
        P("scen", "bldg", None),
        P("scen", None),
        P("scen", None, None),
        P("scen", "bldg", None),
        P("scen", "bldg", None),
        P("bldg", None, None),
        P("bldg", None),
        P("scen"),
        P(None, "scen"),
        P("bldg"),
        P(),
    )
    out_specs = (P("scen", "bldg", None), P("scen", "bldg", None), P("scen", None, None))
    return jax.shard_map(
        per_device, mesh=mesh, in_specs=in_specs, out_specs=out_specs, check_vma=False
    )
```

```python
import functools

import jax
import jax.numpy as jnp
from jax import lax
from jax.experimental import pallas as pl
from jax.experimental.pallas import tpu as pltpu
from jax.sharding import PartitionSpec as P

FEED = 128
PROX = 12
COARSE = 8
LANES = 128
MESH = pl.DeviceIdType.MESH
BF16 = jnp.bfloat16
F32 = jnp.float32


def round_up(value, unit):
    return (value + unit - 1) // unit * unit


def split3(value):
    first = value.astype(BF16)
    rest = value - first.astype(F32)
    second = rest.astype(BF16)
    third = (rest - second.astype(F32)).astype(BF16)
    return first, second, third


def solve_kernel(
    nodes, scen_size, bldg_size,
    demand_hbm, mult_hbm, prev_hbm, inv_hbm, tariff_hbm, price_hbm, limit_hbm, feeder_hbm, weight_hbm, tree_hbm,
    mine_ref, back_ref, full_ref, total_ref,
    demand, mult, prev, inv, tariff, price, limit, feeder, weight, tree,
    send, landed, keep, table, table_landed, hot, factor, cap, w_ref, fixed_ref, z_ref, u_ref, both_ref,
    packed, sums, sums_landed, theirs, load, load_other, load_sent, load_first, load_mine, load_landed,
    in_sem, inv_sem, small_sem, send_sem, recv_sem, table_send, table_recv,
    rs_send, rs_recv, ag_send, ag_recv, on_send, on_recv,
    plan_send, plan_recv, pair_send, pair_recv, load_send, load_recv,
):
    scen, slots, count = demand.shape
    half = count // 2
    wide = 2 * scen
    groups, group_rows = sums.shape[:2]
    size = half // groups
    feeders = price.shape[1]
    pieces = in_sem.shape[0]
    each = scen // pieces
    inv_pieces = inv_sem.shape[0]
    inv_each = slots // inv_pieces
    length = slots // 4
    chips = scen_size // 2
    chunk = group_rows // chips
    me, column = lax.axis_index("scen"), lax.axis_index("bldg")
    core = lax.rem(me, 2)
    chip = lax.div(me, 2)
    partner = (me + 1 - 2 * core, column)
    peers = [(lax.rem(me + 2 * k, scen_size), column) for k in range(1, chips)]
    beside = [(me, lax.rem(column + k, bldg_size)) for k in range(1, bldg_size)]
    own_lanes = pl.ds(pl.multiple_of(core * half, LANES), half)
    away_lanes = pl.ds(pl.multiple_of(half - core * half, LANES), half)

    def described(src, dst, send, recv, device):
        return pltpu.make_async_remote_copy(
            src_ref=src, dst_ref=dst, send_sem=send, recv_sem=recv, device_id=device, device_id_type=MESH
        )

    def remote(*args):
        copy = described(*args)
        copy.start()
        return copy

    def local(src, dst, sem):
        copy = pltpu.make_async_copy(src, dst, sem)
        copy.start()
        return copy

    barrier = pltpu.get_barrier_semaphore()
    for peer in [partner] + peers + beside:
        pl.semaphore_signal(barrier, inc=1, device_id=peer, device_id_type=MESH)
    small = [
        local(src, dst, small_sem.at[k])
        for k, (src, dst) in enumerate((
            (tariff_hbm, tariff), (price_hbm, price), (limit_hbm, limit),
            (feeder_hbm, feeder), (weight_hbm, weight), (tree_hbm, tree),
        ))
    ]
    loads = []
    for p in range(pieces):
        rows = pl.ds(p * each, each)
        loads.append([
            local(src.at[rows], dst.at[rows], in_sem.at[p, k])
            for k, (src, dst) in enumerate(((prev_hbm, prev), (demand_hbm, demand), (mult_hbm, mult)))
        ])
    for p in range(inv_pieces):
        rows = pl.ds(p * inv_each, inv_each)
        local(inv_hbm.at[rows, :, own_lanes], inv.at[rows], inv_sem.at[p])

    for copy in small:
        copy.wait()
    padded = table.shape[0]
    row = lax.broadcasted_iota(jnp.int32, (padded, scen), 0)
    hit = (row == 0) | (row == tree[0:1, :] + 1) | (row == tree[1:2, :] + (1 + COARSE))
    table[...] = jnp.where(hit, weight[...], 0.0)
    one = lax.broadcasted_iota(jnp.int32, (feeders, count), 0) == feeder[...]
    one = one.astype(F32).astype(BF16)
    for k in range(3):
        hot[k * feeders : (k + 1) * feeders, :] = one
    pl.semaphore_wait(barrier, chips + bldg_size - 1)
    table_copy = remote(table, table_landed, table_send, table_recv, partner)

    def fill(s, lanes, into):
        terms = jnp.concatenate(split3(price[s] + tariff[pl.ds(s, 1), :]), axis=0)
        paid = lax.dot_general(terms, hot[:, lanes], (((0,), (0,)), ((), ())), preferred_element_type=F32)
        before = prev[s, :, lanes]
        into[0, s] = 0.5 * before - (paid - demand[s, :, lanes]) - mult[s, :, lanes]
        into[1, s] = jnp.clip(before, 0.0, limit[:, lanes])

    swaps = []
    for p in range(pieces):
        for copy in loads[p]:
            copy.wait()
        for s in range(p * each, (p + 1) * each):
            fill(s, away_lanes, send)
        rows = pl.ds(p * each, each)
        swaps.append(remote(send.at[:, rows], landed.at[:, rows], send_sem.at[p], recv_sem.at[p], partner))
    for s in range(scen):
        fill(s, own_lanes, keep)

    def begin(k, source):
        fixed = jnp.transpose(source[0], (2, 0, 1))
        right = jnp.transpose(source[1], (2, 0, 1)) + fixed
        high = right.astype(BF16)
        fixed_ref[:, k * scen : (k + 1) * scen, :] = fixed
        both_ref[:, k * scen : (k + 1) * scen, :] = high
        both_ref[:, wide + k * scen : wide + (k + 1) * scen, :] = (right - high.astype(F32)).astype(BF16)

    begin(0, keep)
    cap[...] = jnp.transpose(limit[:, own_lanes], (1, 0))
    u_ref[...] = jnp.zeros_like(u_ref)

    def turn(p, carry):
        rows = pl.ds(pl.multiple_of(p * inv_each, inv_each), inv_each)
        pltpu.make_async_copy(inv_hbm.at[rows, :, own_lanes], inv.at[rows], inv_sem.at[p]).wait()
        exact = jnp.transpose(inv[rows], (2, 0, 1))
        high = exact.astype(BF16)
        w_ref[:, rows, :slots] = high
        w_ref[:, rows, LANES : LANES + slots] = (exact - high.astype(F32)).astype(BF16)
        return carry

    lax.fori_loop(0, inv_pieces, turn, 0)
    table_copy.wait()
    lane = lax.broadcasted_iota(jnp.int32, (padded, LANES), 1)
    for s in range(scen):
        factor[s] = jnp.where(lane < size, table[:, s : s + 1], table_landed[:, s : s + 1])
    for copy in swaps:
        copy.wait_recv()
    begin(1, landed)

    def step(b):
        out = jnp.dot(both_ref[b], w_ref[b], preferred_element_type=F32)
        primal = out[:wide, :slots] + (out[:wide, LANES : LANES + slots] + out[wide:, :slots])
        moved = primal + u_ref[b]
        fresh = jnp.clip(moved, 0.0, cap[b : b + 1, :])
        dual = moved - fresh
        right = fresh - dual + fixed_ref[b]
        high = right.astype(BF16)
        z_ref[b] = fresh
        u_ref[b] = dual
        both_ref[b, :wide] = high
        both_ref[b, wide:] = (right - high.astype(F32)).astype(BF16)

    low_lanes = lax.broadcasted_iota(jnp.int32, (length, LANES), 1) < size
    tail = (nodes + 1) // 2 * length

    def add_up(g):
        part = slice(g * size, (g + 1) * size)
        packed[g] = jnp.concatenate(
            [
                jnp.transpose(z_ref[part, :scen, :], (1, 0, 2)),
                jnp.transpose(z_ref[part, scen:, :], (1, 0, 2)),
            ],
            axis=1,
        ).swapaxes(1, 2)
        lanes = pl.ds(pl.multiple_of(core * half, LANES), half)
        member = hot[:feeders, lanes].astype(F32)
        other = pltpu.roll(member, size, 1)
        lower = lax.broadcasted_iota(jnp.int32, (feeders, half), 1) < size
        mine, theirs = (member, other) if g == 0 else (other, member)
        pick = jnp.concatenate(
            [jnp.where(lower, mine, 0.0), jnp.where(lower, 0.0, theirs)], axis=0
        ).astype(BF16)
        for s in range(scen):
            value = packed[g, s]
            high = value.astype(BF16)
            terms = jnp.concatenate([high, (value - high.astype(F32)).astype(BF16)], axis=0)
            out = lax.dot_general(pick, terms, (((1,), (1,)), ((), ())), preferred_element_type=F32)
            out = out[:, :slots] + out[:, slots:]
            for k, into in enumerate((load, load_other)):
                rows = slice(s * feeders, (s + 1) * feeders)
                part_out = out[k * feeders : (k + 1) * feeders]
                into[rows, :] = part_out if g == 0 else into[rows, :] + part_out
        if g == groups - 1:
            load_sent[...] = jnp.transpose(load_other[...], (1, 0))
            pair_load().start()

    def add_nodes(g):
        whole = []
        for n in range(nodes):
            level = 0 if n == 0 else (1 if n <= COARSE else 2)
            acc = jnp.zeros((length, LANES), F32)
            for s in range(scen):
                acc = acc + factor[s, n : n + 1, :] * packed[g, s, level * length : (level + 1) * length, :]
            whole.append(acc + pltpu.roll(acc, size, 1))
            if n % 2 == 1 or n == nodes - 1:
                both = jnp.where(low_lanes, whole[n - n % 2], whole[n])
                sums[g, n // 2 * length : (n // 2 + 1) * length, :] = both
        rest = group_rows - tail
        counted = jnp.sum(table[...] + table_landed[...], axis=1, keepdims=True)
        sums[g, tail : tail + padded, :] = jnp.broadcast_to(counted, (padded, LANES))
        if rest > padded:
            sums[g, tail + padded :, :] = jnp.zeros((rest - padded, LANES), F32)

    def rows_of(index):
        return pl.ds(pl.multiple_of(index * chunk, 8), chunk)

    def spot(g, k):
        return full_ref.at[core, g, rows_of(lax.rem(chip - k + chips, chips))]

    def scatter(g):
        return [
            described(
                sums.at[g, rows_of(lax.div(peer[0], 2))], sums_landed.at[g, k],
                rs_send.at[g, k], rs_recv.at[g, k], peer,
            )
            for k, peer in enumerate(peers)
        ]

    def gather(g):
        return [
            described(spot(g, 0), spot(g, 0), ag_send.at[g, k], ag_recv.at[g, k], peer)
            for k, peer in enumerate(peers)
        ]

    def onward(g, k):
        return described(spot(g, k), spot(g, k), on_send.at[g, k], on_recv.at[g, k], partner)

    def reduce_chunk(g):
        for copy in scatter(g):
            copy.wait_recv()
        acc = sums[g, rows_of(chip), :]
        for k in range(chips - 1):
            acc = acc + sums_landed[g, k]
        full_ref[core, g, rows_of(chip), :] = acc
        for copy in gather(g):
            copy.start()
        onward(g, 0).start()

    def pass_on(g):
        for k, copy in enumerate(gather(g)):
            copy.wait_recv()
            onward(g, k + 1).start()

    def pair_load():
        return described(load_sent, load_first, pair_send, pair_recv, partner)

    turns = PROX // 2
    for g in range(groups):

        def twice(i, carry, g=g):
            if g > 0:
                pl.when(i == turns // 2)(functools.partial(reduce_chunk, g - 1))
                pl.when(i == turns - 1)(functools.partial(pass_on, g - 1))
            for _ in range(2):
                for b in range(g * size, (g + 1) * size):
                    step(b)
            return carry

        lax.fori_loop(0, turns, twice, 0)
        add_up(g)
        add_nodes(g)
        for copy in scatter(g):
            copy.start()

    pair_load().wait_recv()
    load_mine[...] = jnp.transpose(load[...], (1, 0)) + load_first[...]
    load_copies = [
        remote(load_mine, load_landed.at[k], load_send.at[k], load_recv.at[k], peer)
        for k, peer in enumerate(beside)
    ]
    low_half = lax.broadcasted_iota(jnp.int32, (slots, LANES), 1) < size

    def unpack(s, carry):
        first, second = packed[0, s], packed[1, s]
        theirs[s] = jnp.where(low_half, pltpu.roll(first, size, 1), second)
        mine_ref[s] = jnp.where(low_half, first, pltpu.roll(second, size, 1))
        return carry

    lax.fori_loop(0, scen, unpack, 0)
    plan_copy = remote(theirs, back_ref, plan_send, plan_recv, partner)
    last = groups - 1
    reduce_chunk(last)
    pass_on(last)
    total = load_mine[...]
    for k, copy in enumerate(load_copies):
        copy.wait_recv()
        total = total + load_landed[k]
    total_ref[...] = jnp.transpose(total, (1, 0))
    plan_copy.wait_recv()
    sent = swaps + load_copies + [plan_copy, pair_load()]
    for g in range(groups):
        passed = [onward(g, k) for k in range(chips)]
        for copy in passed:
            copy.wait_recv()
        sent = sent + scatter(g) + gather(g) + passed
    for copy in sent:
        copy.wait_send()


def solve(demand, mult, prev, inverse, tariff, price, limit, feeder, weights, tree, nodes, groups, rows):
    scen_size, bldg_size = lax.axis_size("scen"), lax.axis_size("bldg")
    chips = scen_size // 2
    scen, slots, count = demand.shape
    feeders = price.shape[1]
    half = count // 2
    length = slots // 4
    padded = round_up(nodes, 8)
    chunk = rows // chips
    vmem = pl.BlockSpec(memory_space=pltpu.VMEM)
    hbm = pl.BlockSpec(memory_space=pltpu.HBM)
    dma = pltpu.SemaphoreType.DMA
    big = pltpu.VMEM(demand.shape, F32)
    pair = pltpu.VMEM((2, scen, slots, half), F32)
    state = pltpu.VMEM((half, 2 * scen, slots), F32)
    held = lambda array: pltpu.VMEM(array.shape, array.dtype)
    flat = pltpu.VMEM((scen * feeders, slots), F32)
    loads = pltpu.VMEM((slots, scen * feeders), F32)
    return pl.pallas_call(
        functools.partial(solve_kernel, nodes, scen_size, bldg_size),
        in_specs=[hbm] * 10,
        out_specs=[vmem] * 4,
        out_shape=[
            jax.ShapeDtypeStruct((scen, slots, half), F32),
            jax.ShapeDtypeStruct((scen, slots, half), F32),
            jax.ShapeDtypeStruct((2, groups, rows, half), F32),
            jax.ShapeDtypeStruct((scen * feeders, slots), F32),
        ],
        scratch_shapes=[
            big, big, big,
            pltpu.VMEM((slots, slots, half), F32),
            held(tariff), held(price), held(limit), held(feeder), held(weights), held(tree),
            pair, pair, pair,
            pltpu.VMEM((padded, scen), F32), pltpu.VMEM((padded, scen), F32),
            pltpu.VMEM((3 * feeders, count), BF16),
            pltpu.VMEM((scen, padded, LANES), F32),
            pltpu.VMEM((half, slots), F32),
            pltpu.VMEM((half, slots, 2 * LANES), BF16),
            state, state, state,
            pltpu.VMEM((half, 4 * scen, slots), BF16),
            pltpu.VMEM((groups, scen, slots, LANES), F32),
            pltpu.VMEM((groups, rows, LANES), F32),
            pltpu.VMEM((groups, chips - 1, chunk, LANES), F32),
            pltpu.VMEM((scen, slots, half), F32),
            flat, flat, loads, loads, loads,
            pltpu.VMEM((bldg_size - 1, slots, scen * feeders), F32),
            dma((4, 3)), dma((slots // 16,)), dma((6,)), dma((4,)), dma((4,)), dma(()), dma(()),
            dma((groups, chips - 1)), dma((groups, chips - 1)),
            dma((groups, chips - 1)), dma((groups, chips - 1)),
            dma((groups, chips)), dma((groups, chips)),
            dma(()), dma(()), dma(()), dma(()),
            dma((bldg_size - 1,)), dma((bldg_size - 1,)),
        ],
        compiler_params=pltpu.CompilerParams(
            collective_id=0, has_side_effects=True, vmem_limit_bytes=42 * 2**20
        ),
        name="solve",
    )(*(pltpu.with_memory_space_constraint(x, pltpu.HBM) for x in (
        demand, mult, prev, inverse, tariff, price, limit, feeder, weights, tree)))


def spread_kernel(
    nodes, tree_ref, full_ref, mine_ref, back_ref, mult_ref, price_ref, load_ref, limit_ref,
    plan_ref, out_ref, new_price_ref, mean_ref,
):
    step = pl.program_id(0)
    each, slots, count = mult_ref.shape
    half = count // 2
    length = slots // 4
    tail = (nodes + 1) // 2 * length
    groups = full_ref.shape[1]
    size = half // groups
    core = lax.rem(lax.axis_index("scen"), 2)

    @pl.when(step == 0)
    def _():
        low_lanes = lax.broadcasted_iota(jnp.int32, (length, half), 1) < size
        for c in range(2):
            for n in range(nodes):
                count_row = full_ref[c, 0, tail + n : tail + n + 1, :]
                block = slice(n // 2 * length, (n // 2 + 1) * length)
                first = full_ref[c, 0, block, :]
                second = full_ref[c, 1, block, :]
                if n % 2 == 0:
                    share = jnp.where(low_lanes, first, pltpu.roll(second, size, 1))
                else:
                    share = jnp.where(low_lanes, pltpu.roll(first, size, 1), second)
                mean_ref[n, :, c * half : (c + 1) * half] = share / count_row

    for j in range(each):
        s = step * each + j
        places = (0, tree_ref[0, s] + 1, tree_ref[1, s] + (1 + COARSE))
        for source, offset in ((mine_ref, core * half), (back_ref, half - core * half)):
            lanes = pl.ds(pl.multiple_of(offset, LANES), half)
            plan_ref[j, :, lanes] = source[j]
            for level in range(4):
                part = slice(level * length, (level + 1) * length)
                plan = source[j, part, :]
                mean = plan if level == 3 else mean_ref[places[level], :, lanes]
                out_ref[j, part, lanes] = mult_ref[j, part, lanes] + 0.5 * (plan - mean)
    new_price_ref[...] = jnp.maximum(0.0, price_ref[...] + (load_ref[...] - limit_ref[...][None]) / FEED)


def spread(tree, full, mine, back, mult, price, load, limit, nodes):
    scen, slots, count = mult.shape
    feeders = price.shape[1]
    each = 4
    block = lambda *shape: pl.BlockSpec((each,) + shape, lambda i: (i, 0, 0))
    return pl.pallas_call(
        functools.partial(spread_kernel, nodes),
        grid=(scen // each,),
        in_specs=[
            pl.BlockSpec(memory_space=pltpu.SMEM),
            pl.BlockSpec(full.shape, lambda i: (0, 0, 0, 0)),
            block(slots, count // 2), block(slots, count // 2), block(slots, count),
            block(feeders, slots), block(feeders, slots),
            pl.BlockSpec(limit.shape, lambda i: (0, 0)),
        ],
        out_specs=[block(slots, count), block(slots, count), block(feeders, slots)],
        out_shape=[
            jax.ShapeDtypeStruct(mult.shape, F32),
            jax.ShapeDtypeStruct(mult.shape, F32),
            jax.ShapeDtypeStruct(price.shape, F32),
        ],
        scratch_shapes=[pltpu.VMEM((nodes, slots // 4, count), F32)],
        compiler_params=pltpu.CompilerParams(vmem_limit_bytes=24 * 2**20),
        name="spread",
    )(tree, full, mine, back, mult, price, load, limit)


def per_device(
    demand,
    tariff,
    feeder_price,
    multiplier,
    previous_mean,
    inverse,
    power_limit,
    weights,
    tree_node,
    building_feeder,
    feeder_limit,
):
    scen_size = lax.axis_size("scen")
    scen, count, slots = demand.shape
    nodes = 1 + COARSE + scen_size * scen // 8
    groups = 2
    rows = round_up((nodes + 1) // 2 * (slots // 4) + round_up(nodes, 8), 8 * (scen_size // 2))

    def turned(value):
        return jnp.transpose(value, (0, 2, 1))

    limit = jnp.transpose(power_limit, (1, 0))
    mult = turned(multiplier)
    mine, back, full, total = solve(
        turned(demand), mult, turned(previous_mean), jnp.transpose(inverse, (1, 2, 0)), tariff, feeder_price,
        limit, building_feeder.reshape(1, count), weights.reshape(1, scen), tree_node, nodes, groups, rows,
    )
    plan, new_multiplier, new_price = spread(
        tree_node, full, mine, back, mult, feeder_price, total.reshape(feeder_price.shape), feeder_limit, nodes
    )
    return turned(plan), turned(new_multiplier), new_price


def solution(mesh):
    in_specs = (
        P("scen", "bldg", None),
        P("scen", None),
        P("scen", None, None),
        P("scen", "bldg", None),
        P("scen", "bldg", None),
        P("bldg", None, None),
        P("bldg", None),
        P("scen"),
        P(None, "scen"),
        P("bldg"),
        P(),
    )
    out_specs = (P("scen", "bldg", None), P("scen", "bldg", None), P("scen", None, None))
    return jax.shard_map(
        per_device, mesh=mesh, in_specs=in_specs, out_specs=out_specs, check_vma=False
    )
```

```python
import functools

import jax
import jax.numpy as jnp
from jax import lax
from jax.experimental import pallas as pl
from jax.experimental.pallas import tpu as pltpu
from jax.sharding import PartitionSpec as P

FEED = 128
PROX = 12
COARSE = 8
LANES = 128
MESH = pl.DeviceIdType.MESH
BF16 = jnp.bfloat16
F32 = jnp.float32


def round_up(value, unit):
    return (value + unit - 1) // unit * unit


def split3(value):
    first = value.astype(BF16)
    rest = value - first.astype(F32)
    second = rest.astype(BF16)
    third = (rest - second.astype(F32)).astype(BF16)
    return first, second, third


def solve_kernel(
    nodes, scen_size, bldg_size,
    demand_hbm, mult_hbm, prev_hbm, inv_hbm, tariff_hbm, price_hbm, limit_hbm, feeder_hbm, weight_hbm, tree_hbm,
    mine_ref, back_ref, full_ref, total_ref,
    demand, mult, prev, inv, tariff, price, limit, feeder, weight, tree,
    send, landed, keep, table, table_landed, hot, factor, cap, w_ref, fixed_ref, z_ref, u_ref, both_ref,
    packed, sums, sums_landed, theirs, load, load_other, load_sent, load_first, load_mine, load_landed,
    in_sem, inv_sem, small_sem, send_sem, recv_sem, table_send, table_recv,
    rs_send, rs_recv, ag_send, ag_recv, on_send, on_recv,
    plan_send, plan_recv, pair_send, pair_recv, load_send, load_recv,
):
    scen, slots, count = demand.shape
    half = count // 2
    wide = 2 * scen
    groups = sums.shape[0]
    size = half // groups
    feeders = price.shape[1]
    pieces = in_sem.shape[0]
    each = scen // pieces
    inv_pieces = inv_sem.shape[0]
    inv_each = slots // inv_pieces
    length = slots // 4
    chips = scen_size // 2
    pairs = (nodes + 1) // 2
    unit = 8 * chips
    group_rows = [sums.shape[1]] + [round_up(pairs * length, unit)] * (groups - 1)
    me, column = lax.axis_index("scen"), lax.axis_index("bldg")
    core = lax.rem(me, 2)
    chip = lax.div(me, 2)
    partner = (me + 1 - 2 * core, column)
    peers = [(lax.rem(me + 2 * k, scen_size), column) for k in range(1, chips)]
    beside = [(me, lax.rem(column + k, bldg_size)) for k in range(1, bldg_size)]
    own_lanes = pl.ds(pl.multiple_of(core * half, LANES), half)
    away_lanes = pl.ds(pl.multiple_of(half - core * half, LANES), half)

    def described(src, dst, send, recv, device):
        return pltpu.make_async_remote_copy(
            src_ref=src, dst_ref=dst, send_sem=send, recv_sem=recv, device_id=device, device_id_type=MESH
        )

    def remote(*args):
        copy = described(*args)
        copy.start()
        return copy

    def local(src, dst, sem):
        copy = pltpu.make_async_copy(src, dst, sem)
        copy.start()
        return copy

    barrier = pltpu.get_barrier_semaphore()
    for peer in [partner] + peers + beside:
        pl.semaphore_signal(barrier, inc=1, device_id=peer, device_id_type=MESH)
    small = [
        local(src, dst, small_sem.at[k])
        for k, (src, dst) in enumerate((
            (tariff_hbm, tariff), (price_hbm, price), (limit_hbm, limit),
            (feeder_hbm, feeder), (weight_hbm, weight), (tree_hbm, tree),
        ))
    ]
    loads = []
    for p in range(pieces):
        rows = pl.ds(p * each, each)
        loads.append([
            local(src.at[rows], dst.at[rows], in_sem.at[p, k])
            for k, (src, dst) in enumerate(((prev_hbm, prev), (demand_hbm, demand), (mult_hbm, mult)))
        ])
    for p in range(inv_pieces):
        rows = pl.ds(p * inv_each, inv_each)
        local(inv_hbm.at[rows, :, own_lanes], inv.at[rows], inv_sem.at[p])

    for copy in small:
        copy.wait()
    padded = table.shape[0]
    row = lax.broadcasted_iota(jnp.int32, (padded, scen), 0)
    hit = (row == 0) | (row == tree[0:1, :] + 1) | (row == tree[1:2, :] + (1 + COARSE))
    table[...] = jnp.where(hit, weight[...], 0.0)
    one = lax.broadcasted_iota(jnp.int32, (feeders, count), 0) == feeder[...]
    one = one.astype(F32).astype(BF16)
    for k in range(3):
        hot[k * feeders : (k + 1) * feeders, :] = one
    pl.semaphore_wait(barrier, chips + bldg_size - 1)
    table_copy = remote(table, table_landed, table_send, table_recv, partner)

    def fill(s, lanes, into):
        terms = jnp.concatenate(split3(price[s] + tariff[pl.ds(s, 1), :]), axis=0)
        paid = lax.dot_general(terms, hot[:, lanes], (((0,), (0,)), ((), ())), preferred_element_type=F32)
        before = prev[s, :, lanes]
        into[0, s] = 0.5 * before - (paid - demand[s, :, lanes]) - mult[s, :, lanes]
        into[1, s] = jnp.clip(before, 0.0, limit[:, lanes])

    swaps = []
    for p in range(pieces):
        for copy in loads[p]:
            copy.wait()
        for s in range(p * each, (p + 1) * each):
            fill(s, away_lanes, send)
        rows = pl.ds(p * each, each)
        swaps.append(remote(send.at[:, rows], landed.at[:, rows], send_sem.at[p], recv_sem.at[p], partner))
    for s in range(scen):
        fill(s, own_lanes, keep)

    def begin(k, source):
        fixed = jnp.transpose(source[0], (2, 0, 1))
        right = jnp.transpose(source[1], (2, 0, 1)) + fixed
        high = right.astype(BF16)
        fixed_ref[:, k * scen : (k + 1) * scen, :] = fixed
        both_ref[:, k * scen : (k + 1) * scen, :] = high
        both_ref[:, wide + k * scen : wide + (k + 1) * scen, :] = (right - high.astype(F32)).astype(BF16)

    begin(0, keep)
    cap[...] = jnp.transpose(limit[:, own_lanes], (1, 0))
    u_ref[...] = jnp.zeros_like(u_ref)

    def turn(p, carry):
        rows = pl.ds(pl.multiple_of(p * inv_each, inv_each), inv_each)
        pltpu.make_async_copy(inv_hbm.at[rows, :, own_lanes], inv.at[rows], inv_sem.at[p]).wait()
        exact = jnp.transpose(inv[rows], (2, 0, 1))
        high = exact.astype(BF16)
        w_ref[:, rows, :slots] = high
        w_ref[:, rows, LANES : LANES + slots] = (exact - high.astype(F32)).astype(BF16)
        return carry

    lax.fori_loop(0, inv_pieces, turn, 0)
    table_copy.wait()
    lane = lax.broadcasted_iota(jnp.int32, (padded, LANES), 1)
    for s in range(scen):
        factor[s] = jnp.where(lane < size, table[:, s : s + 1], table_landed[:, s : s + 1])
    for copy in swaps:
        copy.wait_recv()
    begin(1, landed)

    def step(b):
        out = jnp.dot(both_ref[b], w_ref[b], preferred_element_type=F32)
        primal = out[:wide, :slots] + (out[:wide, LANES : LANES + slots] + out[wide:, :slots])
        moved = primal + u_ref[b]
        fresh = jnp.clip(moved, 0.0, cap[b : b + 1, :])
        dual = moved - fresh
        right = fresh - dual + fixed_ref[b]
        high = right.astype(BF16)
        z_ref[b] = fresh
        u_ref[b] = dual
        both_ref[b, :wide] = high
        both_ref[b, wide:] = (right - high.astype(F32)).astype(BF16)

    low_lanes = lax.broadcasted_iota(jnp.int32, (length, LANES), 1) < size
    tail = (nodes + 1) // 2 * length

    def add_up(g):
        part = slice(g * size, (g + 1) * size)
        turned = [jnp.transpose(z_ref[part, k * scen : (k + 1) * scen, :], (1, 0, 2)) for k in range(2)]
        lanes = pl.ds(pl.multiple_of(core * half, LANES), half)
        member = hot[:feeders, lanes].astype(F32)
        pick = (member if g == 0 else pltpu.roll(member, size, 1))[:, :size].astype(BF16)
        for k, into in ((1, load_other), (0, load)):
            for s in range(scen):
                value = turned[k][s]
                high = value.astype(BF16)
                low = (value - high.astype(F32)).astype(BF16)
                out = jnp.dot(pick, high, preferred_element_type=F32) + jnp.dot(
                    pick, low, preferred_element_type=F32
                )
                rows = slice(s * feeders, (s + 1) * feeders)
                into[rows, :] = out if g == 0 else into[rows, :] + out
        if g == groups - 1:
            load_sent[...] = jnp.transpose(load_other[...], (1, 0))
            pair_load().start()
        packed[g] = jnp.concatenate(turned, axis=1).swapaxes(1, 2)

    def add_nodes(g):
        whole = []
        for n in range(nodes):
            level = 0 if n == 0 else (1 if n <= COARSE else 2)
            acc = jnp.zeros((length, LANES), F32)
            for s in range(scen):
                acc = acc + factor[s, n : n + 1, :] * packed[g, s, level * length : (level + 1) * length, :]
            whole.append(acc + pltpu.roll(acc, size, 1))
            if n % 2 == 1 or n == nodes - 1:
                both = jnp.where(low_lanes, whole[n - n % 2], whole[n])
                sums[g, n // 2 * length : (n // 2 + 1) * length, :] = both
        rest = group_rows[g] - tail
        if g > 0:
            if rest > 0:
                sums[g, tail : tail + rest, :] = jnp.zeros((rest, LANES), F32)
            return
        counted = jnp.sum(table[...] + table_landed[...], axis=1, keepdims=True)
        sums[g, tail : tail + padded, :] = jnp.broadcast_to(counted, (padded, LANES))
        if rest > padded:
            sums[g, tail + padded : tail + rest, :] = jnp.zeros((rest - padded, LANES), F32)

    def rows_of(g, index):
        chunk = group_rows[g] // chips
        return pl.ds(pl.multiple_of(index * chunk, 8), chunk)

    def spot(g, k):
        return full_ref.at[core, g, rows_of(g, lax.rem(chip - k + chips, chips))]

    def scatter(g):
        return [
            described(
                sums.at[g, rows_of(g, lax.div(peer[0], 2))], sums_landed.at[g, k, pl.ds(0, group_rows[g] // chips)],
                rs_send.at[g, k], rs_recv.at[g, k], peer,
            )
            for k, peer in enumerate(peers)
        ]

    def gather(g):
        return [
            described(spot(g, 0), spot(g, 0), ag_send.at[g, k], ag_recv.at[g, k], peer)
            for k, peer in enumerate(peers)
        ]

    def onward(g, k):
        return described(spot(g, k), spot(g, k), on_send.at[g, k], on_recv.at[g, k], partner)

    def reduce_chunk(g):
        for copy in scatter(g):
            copy.wait_recv()
        acc = sums[g, rows_of(g, chip), :]
        for k in range(chips - 1):
            acc = acc + sums_landed[g, k, : group_rows[g] // chips]
        full_ref[core, g, rows_of(g, chip), :] = acc
        for copy in gather(g):
            copy.start()
        onward(g, 0).start()

    def pass_on(g):
        for k, copy in enumerate(gather(g)):
            copy.wait_recv()
            onward(g, k + 1).start()

    def pair_load():
        return described(load_sent, load_first, pair_send, pair_recv, partner)

    turns = PROX // 2
    for g in range(groups):

        def twice(i, carry, g=g):
            if g > 0:
                pl.when(i == turns // 2)(functools.partial(reduce_chunk, g - 1))
                pl.when(i == turns - 1)(functools.partial(pass_on, g - 1))
            for _ in range(2):
                for b in range(g * size, (g + 1) * size):
                    step(b)
            return carry

        lax.fori_loop(0, turns, twice, 0)
        add_up(g)
        add_nodes(g)
        for copy in scatter(g):
            copy.start()

    pair_load().wait_recv()
    load_mine[...] = jnp.transpose(load[...], (1, 0)) + load_first[...]
    load_copies = [
        remote(load_mine, load_landed.at[k], load_send.at[k], load_recv.at[k], peer)
        for k, peer in enumerate(beside)
    ]
    low_half = lax.broadcasted_iota(jnp.int32, (slots, LANES), 1) < size

    def unpack(s, carry):
        first, second = packed[0, s], packed[1, s]
        theirs[s] = jnp.where(low_half, pltpu.roll(first, size, 1), second)
        mine_ref[s] = jnp.where(low_half, first, pltpu.roll(second, size, 1))
        return carry

    lax.fori_loop(0, scen, unpack, 0)
    plan_copy = remote(theirs, back_ref, plan_send, plan_recv, partner)
    last = groups - 1
    reduce_chunk(last)
    pass_on(last)
    total = load_mine[...]
    for k, copy in enumerate(load_copies):
        copy.wait_recv()
        total = total + load_landed[k]
    total_ref[...] = jnp.transpose(total, (1, 0))
    plan_copy.wait_recv()
    sent = swaps + load_copies + [plan_copy, pair_load()]
    for g in range(groups):
        passed = [onward(g, k) for k in range(chips)]
        for copy in passed:
            copy.wait_recv()
        sent = sent + scatter(g) + gather(g) + passed
    for copy in sent:
        copy.wait_send()


def solve(demand, mult, prev, inverse, tariff, price, limit, feeder, weights, tree, nodes, groups, rows):
    scen_size, bldg_size = lax.axis_size("scen"), lax.axis_size("bldg")
    chips = scen_size // 2
    scen, slots, count = demand.shape
    feeders = price.shape[1]
    half = count // 2
    length = slots // 4
    padded = round_up(nodes, 8)
    chunk = rows // chips
    vmem = pl.BlockSpec(memory_space=pltpu.VMEM)
    hbm = pl.BlockSpec(memory_space=pltpu.HBM)
    dma = pltpu.SemaphoreType.DMA
    big = pltpu.VMEM(demand.shape, F32)
    pair = pltpu.VMEM((2, scen, slots, half), F32)
    state = pltpu.VMEM((half, 2 * scen, slots), F32)
    held = lambda array: pltpu.VMEM(array.shape, array.dtype)
    flat = pltpu.VMEM((scen * feeders, slots), F32)
    loads = pltpu.VMEM((slots, scen * feeders), F32)
    return pl.pallas_call(
        functools.partial(solve_kernel, nodes, scen_size, bldg_size),
        in_specs=[hbm] * 10,
        out_specs=[vmem] * 4,
        out_shape=[
            jax.ShapeDtypeStruct((scen, slots, half), F32),
            jax.ShapeDtypeStruct((scen, slots, half), F32),
            jax.ShapeDtypeStruct((2, groups, rows, half), F32),
            jax.ShapeDtypeStruct((scen * feeders, slots), F32),
        ],
        scratch_shapes=[
            big, big, big,
            pltpu.VMEM((slots, slots, half), F32),
            held(tariff), held(price), held(limit), held(feeder), held(weights), held(tree),
            pair, pair, pair,
            pltpu.VMEM((padded, scen), F32), pltpu.VMEM((padded, scen), F32),
            pltpu.VMEM((3 * feeders, count), BF16),
            pltpu.VMEM((scen, padded, LANES), F32),
            pltpu.VMEM((half, slots), F32),
            pltpu.VMEM((half, slots, 2 * LANES), BF16),
            state, state, state,
            pltpu.VMEM((half, 4 * scen, slots), BF16),
            pltpu.VMEM((groups, scen, slots, LANES), F32),
            pltpu.VMEM((groups, rows, LANES), F32),
            pltpu.VMEM((groups, chips - 1, chunk, LANES), F32),
            pltpu.VMEM((scen, slots, half), F32),
            flat, flat, loads, loads, loads,
            pltpu.VMEM((bldg_size - 1, slots, scen * feeders), F32),
            dma((4, 3)), dma((slots // 16,)), dma((6,)), dma((4,)), dma((4,)), dma(()), dma(()),
            dma((groups, chips - 1)), dma((groups, chips - 1)),
            dma((groups, chips - 1)), dma((groups, chips - 1)),
            dma((groups, chips)), dma((groups, chips)),
            dma(()), dma(()), dma(()), dma(()),
            dma((bldg_size - 1,)), dma((bldg_size - 1,)),
        ],
        compiler_params=pltpu.CompilerParams(
            collective_id=0, has_side_effects=True, vmem_limit_bytes=42 * 2**20
        ),
        name="solve",
    )(*(pltpu.with_memory_space_constraint(x, pltpu.HBM) for x in (
        demand, mult, prev, inverse, tariff, price, limit, feeder, weights, tree)))


def spread_kernel(
    nodes, tree_ref, full_ref, mine_ref, back_ref, mult_ref, price_ref, load_ref, limit_ref,
    plan_hbm, out_hbm, new_price_hbm, mean_ref, out_ref, new_price, plan_sem, out_sem, price_sem,
):
    scen, slots, count = mult_ref.shape
    half = count // 2
    length = slots // 4
    tail = (nodes + 1) // 2 * length
    groups = full_ref.shape[1]
    size = half // groups
    pieces = out_sem.shape[0]
    each = scen // pieces
    core = lax.rem(lax.axis_index("scen"), 2)
    sides = [
        (source, pl.ds(pl.multiple_of(offset, LANES), half))
        for source, offset in ((mine_ref, core * half), (back_ref, half - core * half))
    ]
    copies = []
    for p in range(pieces):
        rows = pl.ds(p * each, each)
        for k, (source, lanes) in enumerate(sides):
            copies.append(pltpu.make_async_copy(source.at[rows], plan_hbm.at[rows, :, lanes], plan_sem.at[p, k]))
            copies[-1].start()
    new_price[...] = jnp.maximum(0.0, price_ref[...] + (load_ref[...] - limit_ref[...][None]) / FEED)
    copies.append(pltpu.make_async_copy(new_price, new_price_hbm, price_sem))
    copies[-1].start()

    low_lanes = lax.broadcasted_iota(jnp.int32, (length, half), 1) < size
    for c in range(2):
        for n in range(nodes):
            count_row = full_ref[c, 0, tail + n : tail + n + 1, :]
            block = slice(n // 2 * length, (n // 2 + 1) * length)
            first = full_ref[c, 0, block, :]
            second = full_ref[c, 1, block, :]
            if n % 2 == 0:
                share = jnp.where(low_lanes, first, pltpu.roll(second, size, 1))
            else:
                share = jnp.where(low_lanes, pltpu.roll(first, size, 1), second)
            mean_ref[n, :, c * half : (c + 1) * half] = share / count_row

    def finish(s, carry):
        places = (0, tree_ref[0, s] + 1, tree_ref[1, s] + (1 + COARSE))
        for source, lanes in sides:
            for level in range(4):
                part = slice(level * length, (level + 1) * length)
                plan = source[s, part, :]
                mean = plan if level == 3 else mean_ref[places[level], :, lanes]
                out_ref[s, part, lanes] = mult_ref[s, part, lanes] + 0.5 * (plan - mean)
        return carry

    for p in range(pieces):
        lax.fori_loop(p * each, (p + 1) * each, finish, 0)
        rows = pl.ds(p * each, each)
        copies.append(pltpu.make_async_copy(out_ref.at[rows], out_hbm.at[rows], out_sem.at[p]))
        copies[-1].start()
    for copy in copies:
        copy.wait()


def spread(tree, full, mine, back, mult, price, load, limit, nodes):
    scen, slots, count = mult.shape
    pieces = 4
    vmem = pl.BlockSpec(memory_space=pltpu.VMEM)
    hbm = pl.BlockSpec(memory_space=pltpu.HBM)
    dma = pltpu.SemaphoreType.DMA
    return pl.pallas_call(
        functools.partial(spread_kernel, nodes),
        in_specs=[pl.BlockSpec(memory_space=pltpu.SMEM)] + [vmem] * 7,
        out_specs=[hbm] * 3,
        out_shape=[
            jax.ShapeDtypeStruct(mult.shape, F32),
            jax.ShapeDtypeStruct(mult.shape, F32),
            jax.ShapeDtypeStruct(price.shape, F32),
        ],
        scratch_shapes=[
            pltpu.VMEM((nodes, slots // 4, count), F32),
            pltpu.VMEM(mult.shape, F32),
            pltpu.VMEM(price.shape, F32),
            dma((pieces, 2)), dma((pieces,)), dma(()),
        ],
        compiler_params=pltpu.CompilerParams(vmem_limit_bytes=24 * 2**20),
        name="spread",
    )(tree, full, mine, back, mult, price, load, limit)


def per_device(
    demand,
    tariff,
    feeder_price,
    multiplier,
    previous_mean,
    inverse,
    power_limit,
    weights,
    tree_node,
    building_feeder,
    feeder_limit,
):
    scen_size = lax.axis_size("scen")
    scen, count, slots = demand.shape
    nodes = 1 + COARSE + scen_size * scen // 8
    groups = 2
    rows = round_up((nodes + 1) // 2 * (slots // 4) + round_up(nodes, 8), 8 * (scen_size // 2))

    def turned(value):
        return jnp.transpose(value, (0, 2, 1))

    limit = jnp.transpose(power_limit, (1, 0))
    mult = turned(multiplier)
    mine, back, full, total = solve(
        turned(demand), mult, turned(previous_mean), jnp.transpose(inverse, (1, 2, 0)), tariff, feeder_price,
        limit, building_feeder.reshape(1, count), weights.reshape(1, scen), tree_node, nodes, groups, rows,
    )
    plan, new_multiplier, new_price = spread(
        tree_node, full, mine, back, mult, feeder_price, total.reshape(feeder_price.shape), feeder_limit, nodes
    )
    return turned(plan), turned(new_multiplier), new_price


def solution(mesh):
    in_specs = (
        P("scen", "bldg", None),
        P("scen", None),
        P("scen", None, None),
        P("scen", "bldg", None),
        P("scen", "bldg", None),
        P("bldg", None, None),
        P("bldg", None),
        P("scen"),
        P(None, "scen"),
        P("bldg"),
        P(),
    )
    out_specs = (P("scen", "bldg", None), P("scen", "bldg", None), P("scen", None, None))
    return jax.shard_map(
        per_device, mesh=mesh, in_specs=in_specs, out_specs=out_specs, check_vma=False
    )
```

```python
import functools

import jax
import jax.numpy as jnp
from jax import lax
from jax.experimental import pallas as pl
from jax.experimental.pallas import tpu as pltpu
from jax.sharding import PartitionSpec as P

FEED = 128
PROX = 12
COARSE = 8
LANES = 128
MESH = pl.DeviceIdType.MESH
BF16 = jnp.bfloat16
F32 = jnp.float32


def round_up(value, unit):
    return (value + unit - 1) // unit * unit


def split3(value):
    first = value.astype(BF16)
    rest = value - first.astype(F32)
    second = rest.astype(BF16)
    third = (rest - second.astype(F32)).astype(BF16)
    return first, second, third


def solve_kernel(
    nodes, scen_size, bldg_size,
    demand_hbm, mult_hbm, prev_hbm, inv_hbm, tariff_hbm, price_hbm, limit_hbm, feeder_hbm, weight_hbm, tree_hbm,
    mine_ref, back_ref, full_ref, total_ref,
    demand, mult, prev, inv, tariff, price, limit, feeder, weight, tree,
    send, landed, keep, table, table_landed, hot, factor, cap, w_ref, fixed_ref, z_ref, u_ref, both_ref,
    packed, sums, sums_landed, theirs, load, load_other, load_sent, load_first, load_mine, load_landed,
    in_sem, inv_sem, small_sem, send_sem, recv_sem, table_send, table_recv,
    rs_send, rs_recv, ag_send, ag_recv, on_send, on_recv,
    plan_send, plan_recv, pair_send, pair_recv, load_send, load_recv,
):
    scen, slots, count = demand.shape
    half = count // 2
    wide = 2 * scen
    groups = sums.shape[0]
    size = half // groups
    feeders = price.shape[1]
    pieces = in_sem.shape[0]
    each = scen // pieces
    inv_pieces = inv_sem.shape[0]
    inv_each = slots // inv_pieces
    length = slots // 4
    chips = scen_size // 2
    pairs = (nodes + 1) // 2
    unit = 8 * chips
    group_rows = [sums.shape[1]] + [round_up(pairs * length, unit)] * (groups - 1)
    me, column = lax.axis_index("scen"), lax.axis_index("bldg")
    core = lax.rem(me, 2)
    chip = lax.div(me, 2)
    partner = (me + 1 - 2 * core, column)
    peers = [(lax.rem(me + 2 * k, scen_size), column) for k in range(1, chips)]
    beside = [(me, lax.rem(column + k, bldg_size)) for k in range(1, bldg_size)]
    own_lanes = pl.ds(pl.multiple_of(core * half, LANES), half)
    away_lanes = pl.ds(pl.multiple_of(half - core * half, LANES), half)

    def described(src, dst, send, recv, device):
        return pltpu.make_async_remote_copy(
            src_ref=src, dst_ref=dst, send_sem=send, recv_sem=recv, device_id=device, device_id_type=MESH
        )

    def remote(*args):
        copy = described(*args)
        copy.start()
        return copy

    def local(src, dst, sem):
        copy = pltpu.make_async_copy(src, dst, sem)
        copy.start()
        return copy

    barrier = pltpu.get_barrier_semaphore()
    for peer in [partner] + peers + beside:
        pl.semaphore_signal(barrier, inc=1, device_id=peer, device_id_type=MESH)
    small = [
        local(src, dst, small_sem.at[k])
        for k, (src, dst) in enumerate((
            (tariff_hbm, tariff), (price_hbm, price), (limit_hbm, limit),
            (feeder_hbm, feeder), (weight_hbm, weight), (tree_hbm, tree),
        ))
    ]
    loads = []
    for p in range(pieces):
        rows = pl.ds(p * each, each)
        loads.append([
            local(src.at[rows], dst.at[rows], in_sem.at[p, k])
            for k, (src, dst) in enumerate(((prev_hbm, prev), (demand_hbm, demand), (mult_hbm, mult)))
        ])
    for p in range(inv_pieces):
        rows = pl.ds(p * inv_each, inv_each)
        local(inv_hbm.at[rows, :, own_lanes], inv.at[rows], inv_sem.at[p])

    for copy in small:
        copy.wait()
    padded = table.shape[0]
    row = lax.broadcasted_iota(jnp.int32, (padded, scen), 0)
    hit = (row == 0) | (row == tree[0:1, :] + 1) | (row == tree[1:2, :] + (1 + COARSE))
    table[...] = jnp.where(hit, weight[...], 0.0)
    one = lax.broadcasted_iota(jnp.int32, (feeders, count), 0) == feeder[...]
    one = one.astype(F32).astype(BF16)
    for k in range(3):
        hot[k * feeders : (k + 1) * feeders, :] = one
    pl.semaphore_wait(barrier, chips + bldg_size - 1)
    table_copy = remote(table, table_landed, table_send, table_recv, partner)

    def fill(s, lanes, into):
        terms = jnp.concatenate(split3(price[s] + tariff[pl.ds(s, 1), :]), axis=0)
        paid = lax.dot_general(terms, hot[:, lanes], (((0,), (0,)), ((), ())), preferred_element_type=F32)
        before = prev[s, :, lanes]
        into[0, s] = 0.5 * before - (paid - demand[s, :, lanes]) - mult[s, :, lanes]
        into[1, s] = jnp.clip(before, 0.0, limit[:, lanes])

    swaps = []
    for p in range(pieces):
        for copy in loads[p]:
            copy.wait()
        for s in range(p * each, (p + 1) * each):
            fill(s, away_lanes, send)
        rows = pl.ds(p * each, each)
        swaps.append(remote(send.at[:, rows], landed.at[:, rows], send_sem.at[p], recv_sem.at[p], partner))
    for s in range(scen):
        fill(s, own_lanes, keep)

    def begin(k, source):
        fixed = jnp.transpose(source[0], (2, 0, 1))
        right = jnp.transpose(source[1], (2, 0, 1)) + fixed
        high = right.astype(BF16)
        fixed_ref[:, k * scen : (k + 1) * scen, :] = fixed
        both_ref[:, k * scen : (k + 1) * scen, :] = high
        both_ref[:, wide + k * scen : wide + (k + 1) * scen, :] = (right - high.astype(F32)).astype(BF16)

    begin(0, keep)
    cap[...] = jnp.transpose(limit[:, own_lanes], (1, 0))
    u_ref[...] = jnp.zeros_like(u_ref)

    def turn(p, carry):
        rows = pl.ds(pl.multiple_of(p * inv_each, inv_each), inv_each)
        pltpu.make_async_copy(inv_hbm.at[rows, :, own_lanes], inv.at[rows], inv_sem.at[p]).wait()
        exact = jnp.transpose(inv[rows], (2, 0, 1))
        high = exact.astype(BF16)
        w_ref[:, rows, :slots] = high
        w_ref[:, rows, LANES : LANES + slots] = (exact - high.astype(F32)).astype(BF16)
        return carry

    lax.fori_loop(0, inv_pieces, turn, 0)
    table_copy.wait()
    lane = lax.broadcasted_iota(jnp.int32, (padded, LANES), 1)
    for s in range(scen):
        factor[s] = jnp.where(lane < size, table[:, s : s + 1], table_landed[:, s : s + 1])
    for copy in swaps:
        copy.wait_recv()
    begin(1, landed)

    def step(b, keep_plan=True):
        out = jnp.dot(both_ref[b], w_ref[b], preferred_element_type=F32)
        primal = out[:wide, :slots] + (out[:wide, LANES : LANES + slots] + out[wide:, :slots])
        moved = primal + u_ref[b]
        fresh = jnp.clip(moved, 0.0, cap[b : b + 1, :])
        dual = moved - fresh
        right = fresh - dual + fixed_ref[b]
        high = right.astype(BF16)
        if keep_plan:
            z_ref[b] = fresh
        u_ref[b] = dual
        both_ref[b, :wide] = high
        both_ref[b, wide:] = (right - high.astype(F32)).astype(BF16)

    low_lanes = lax.broadcasted_iota(jnp.int32, (length, LANES), 1) < size
    tail = (nodes + 1) // 2 * length

    def add_up(g):
        part = slice(g * size, (g + 1) * size)
        turned = [jnp.transpose(z_ref[part, k * scen : (k + 1) * scen, :], (1, 0, 2)) for k in range(2)]
        lanes = pl.ds(pl.multiple_of(core * half, LANES), half)
        member = hot[:feeders, lanes].astype(F32)
        pick = (member if g == 0 else pltpu.roll(member, size, 1))[:, :size].astype(BF16)
        for k, into in ((1, load_other), (0, load)):
            for s in range(scen):
                value = turned[k][s]
                high = value.astype(BF16)
                low = (value - high.astype(F32)).astype(BF16)
                out = jnp.dot(pick, high, preferred_element_type=F32) + jnp.dot(
                    pick, low, preferred_element_type=F32
                )
                rows = slice(s * feeders, (s + 1) * feeders)
                into[rows, :] = out if g == 0 else into[rows, :] + out
        if g == groups - 1:
            load_sent[...] = jnp.transpose(load_other[...], (1, 0))
            pair_load().start()
        packed[g] = jnp.concatenate(turned, axis=1).swapaxes(1, 2)

    def add_nodes(g):
        whole = []
        for n in range(nodes):
            level = 0 if n == 0 else (1 if n <= COARSE else 2)
            acc = jnp.zeros((length, LANES), F32)
            for s in range(scen):
                acc = acc + factor[s, n : n + 1, :] * packed[g, s, level * length : (level + 1) * length, :]
            whole.append(acc + pltpu.roll(acc, size, 1))
            if n % 2 == 1 or n == nodes - 1:
                both = jnp.where(low_lanes, whole[n - n % 2], whole[n])
                sums[g, n // 2 * length : (n // 2 + 1) * length, :] = both
        rest = group_rows[g] - tail
        if g > 0:
            if rest > 0:
                sums[g, tail : tail + rest, :] = jnp.zeros((rest, LANES), F32)
            return
        counted = jnp.sum(table[...] + table_landed[...], axis=1, keepdims=True)
        sums[g, tail : tail + padded, :] = jnp.broadcast_to(counted, (padded, LANES))
        if rest > padded:
            sums[g, tail + padded : tail + rest, :] = jnp.zeros((rest - padded, LANES), F32)

    def rows_of(g, index):
        chunk = group_rows[g] // chips
        return pl.ds(pl.multiple_of(index * chunk, 8), chunk)

    def spot(g, k):
        return full_ref.at[core, g, rows_of(g, lax.rem(chip - k + chips, chips))]

    def scatter(g):
        return [
            described(
                sums.at[g, rows_of(g, lax.div(peer[0], 2))], sums_landed.at[g, k, pl.ds(0, group_rows[g] // chips)],
                rs_send.at[g, k], rs_recv.at[g, k], peer,
            )
            for k, peer in enumerate(peers)
        ]

    def gather(g):
        return [
            described(spot(g, 0), spot(g, 0), ag_send.at[g, k], ag_recv.at[g, k], peer)
            for k, peer in enumerate(peers)
        ]

    def onward(g, k):
        return described(spot(g, k), spot(g, k), on_send.at[g, k], on_recv.at[g, k], partner)

    def reduce_chunk(g):
        for copy in scatter(g):
            copy.wait_recv()
        acc = sums[g, rows_of(g, chip), :]
        for k in range(chips - 1):
            acc = acc + sums_landed[g, k, : group_rows[g] // chips]
        full_ref[core, g, rows_of(g, chip), :] = acc
        for copy in gather(g):
            copy.start()
        onward(g, 0).start()

    def pass_on(g):
        for k, copy in enumerate(gather(g)):
            copy.wait_recv()
            onward(g, k + 1).start()

    def pair_load():
        return described(load_sent, load_first, pair_send, pair_recv, partner)

    turns = PROX // 2
    for g in range(groups):

        def twice(i, carry, g=g):
            if g > 0:
                pl.when(i == turns // 2)(functools.partial(reduce_chunk, g - 1))
                pl.when(i == turns - 1)(functools.partial(pass_on, g - 1))
            for turn_of in range(2):
                for b in range(g * size, (g + 1) * size):
                    step(b, turn_of == 1)
            return carry

        lax.fori_loop(0, turns, twice, 0)
        add_up(g)
        add_nodes(g)
        for copy in scatter(g):
            copy.start()

    pair_load().wait_recv()
    load_mine[...] = jnp.transpose(load[...], (1, 0)) + load_first[...]
    load_copies = [
        remote(load_mine, load_landed.at[k], load_send.at[k], load_recv.at[k], peer)
        for k, peer in enumerate(beside)
    ]
    low_half = lax.broadcasted_iota(jnp.int32, (slots, LANES), 1) < size

    def unpack(s, carry):
        first, second = packed[0, s], packed[1, s]
        theirs[s] = jnp.where(low_half, pltpu.roll(first, size, 1), second)
        mine_ref[s] = jnp.where(low_half, first, pltpu.roll(second, size, 1))
        return carry

    lax.fori_loop(0, scen, unpack, 0)
    plan_copy = remote(theirs, back_ref, plan_send, plan_recv, partner)
    last = groups - 1
    reduce_chunk(last)
    pass_on(last)
    total = load_mine[...]
    for k, copy in enumerate(load_copies):
        copy.wait_recv()
        total = total + load_landed[k]
    total_ref[...] = jnp.transpose(total, (1, 0))
    plan_copy.wait_recv()
    sent = swaps + load_copies + [plan_copy, pair_load()]
    for g in range(groups):
        passed = [onward(g, k) for k in range(chips)]
        for copy in passed:
            copy.wait_recv()
        sent = sent + scatter(g) + gather(g) + passed
    for copy in sent:
        copy.wait_send()


def solve(demand, mult, prev, inverse, tariff, price, limit, feeder, weights, tree, nodes, groups, rows):
    scen_size, bldg_size = lax.axis_size("scen"), lax.axis_size("bldg")
    chips = scen_size // 2
    scen, slots, count = demand.shape
    feeders = price.shape[1]
    half = count // 2
    length = slots // 4
    padded = round_up(nodes, 8)
    chunk = rows // chips
    vmem = pl.BlockSpec(memory_space=pltpu.VMEM)
    hbm = pl.BlockSpec(memory_space=pltpu.HBM)
    dma = pltpu.SemaphoreType.DMA
    big = pltpu.VMEM(demand.shape, F32)
    pair = pltpu.VMEM((2, scen, slots, half), F32)
    state = pltpu.VMEM((half, 2 * scen, slots), F32)
    held = lambda array: pltpu.VMEM(array.shape, array.dtype)
    flat = pltpu.VMEM((scen * feeders, slots), F32)
    loads = pltpu.VMEM((slots, scen * feeders), F32)
    return pl.pallas_call(
        functools.partial(solve_kernel, nodes, scen_size, bldg_size),
        in_specs=[hbm] * 10,
        out_specs=[vmem] * 4,
        out_shape=[
            jax.ShapeDtypeStruct((scen, slots, half), F32),
            jax.ShapeDtypeStruct((scen, slots, half), F32),
            jax.ShapeDtypeStruct((2, groups, rows, half), F32),
            jax.ShapeDtypeStruct((scen * feeders, slots), F32),
        ],
        scratch_shapes=[
            big, big, big,
            pltpu.VMEM((slots, slots, half), F32),
            held(tariff), held(price), held(limit), held(feeder), held(weights), held(tree),
            pair, pair, pair,
            pltpu.VMEM((padded, scen), F32), pltpu.VMEM((padded, scen), F32),
            pltpu.VMEM((3 * feeders, count), BF16),
            pltpu.VMEM((scen, padded, LANES), F32),
            pltpu.VMEM((half, slots), F32),
            pltpu.VMEM((half, slots, 2 * LANES), BF16),
            state, state, state,
            pltpu.VMEM((half, 4 * scen, slots), BF16),
            pltpu.VMEM((groups, scen, slots, LANES), F32),
            pltpu.VMEM((groups, rows, LANES), F32),
            pltpu.VMEM((groups, chips - 1, chunk, LANES), F32),
            pltpu.VMEM((scen, slots, half), F32),
            flat, flat, loads, loads, loads,
            pltpu.VMEM((bldg_size - 1, slots, scen * feeders), F32),
            dma((4, 3)), dma((slots // 16,)), dma((6,)), dma((4,)), dma((4,)), dma(()), dma(()),
            dma((groups, chips - 1)), dma((groups, chips - 1)),
            dma((groups, chips - 1)), dma((groups, chips - 1)),
            dma((groups, chips)), dma((groups, chips)),
            dma(()), dma(()), dma(()), dma(()),
            dma((bldg_size - 1,)), dma((bldg_size - 1,)),
        ],
        compiler_params=pltpu.CompilerParams(
            collective_id=0, has_side_effects=True, vmem_limit_bytes=42 * 2**20,
        ),
        name="solve",
    )(*(pltpu.with_memory_space_constraint(x, pltpu.HBM) for x in (
        demand, mult, prev, inverse, tariff, price, limit, feeder, weights, tree)))


def spread_kernel(
    nodes, tree_ref, full_ref, mine_ref, back_ref, mult_ref, price_ref, load_ref, limit_ref,
    plan_hbm, out_hbm, new_price_hbm, mean_ref, out_ref, new_price, plan_sem, out_sem, price_sem,
):
    scen, slots, count = mult_ref.shape
    half = count // 2
    length = slots // 4
    tail = (nodes + 1) // 2 * length
    groups = full_ref.shape[1]
    size = half // groups
    pieces = out_sem.shape[0]
    each = scen // pieces
    core = lax.rem(lax.axis_index("scen"), 2)
    sides = [
        (source, pl.ds(pl.multiple_of(offset, LANES), half))
        for source, offset in ((mine_ref, core * half), (back_ref, half - core * half))
    ]
    copies = []
    for p in range(pieces):
        rows = pl.ds(p * each, each)
        for k, (source, lanes) in enumerate(sides):
            copies.append(pltpu.make_async_copy(source.at[rows], plan_hbm.at[rows, :, lanes], plan_sem.at[p, k]))
            copies[-1].start()
    new_price[...] = jnp.maximum(0.0, price_ref[...] + (load_ref[...] - limit_ref[...][None]) / FEED)
    copies.append(pltpu.make_async_copy(new_price, new_price_hbm, price_sem))
    copies[-1].start()

    low_lanes = lax.broadcasted_iota(jnp.int32, (length, half), 1) < size
    for c in range(2):
        for n in range(nodes):
            count_row = full_ref[c, 0, tail + n : tail + n + 1, :]
            block = slice(n // 2 * length, (n // 2 + 1) * length)
            first = full_ref[c, 0, block, :]
            second = full_ref[c, 1, block, :]
            if n % 2 == 0:
                share = jnp.where(low_lanes, first, pltpu.roll(second, size, 1))
            else:
                share = jnp.where(low_lanes, pltpu.roll(first, size, 1), second)
            mean_ref[n, :, c * half : (c + 1) * half] = share / count_row

    def finish(s, carry):
        places = (0, tree_ref[0, s] + 1, tree_ref[1, s] + (1 + COARSE))
        for source, lanes in sides:
            for level in range(4):
                part = slice(level * length, (level + 1) * length)
                plan = source[s, part, :]
                mean = plan if level == 3 else mean_ref[places[level], :, lanes]
                out_ref[s, part, lanes] = mult_ref[s, part, lanes] + 0.5 * (plan - mean)
        return carry

    for p in range(pieces):
        lax.fori_loop(p * each, (p + 1) * each, finish, 0)
        rows = pl.ds(p * each, each)
        copies.append(pltpu.make_async_copy(out_ref.at[rows], out_hbm.at[rows], out_sem.at[p]))
        copies[-1].start()
    for copy in copies:
        copy.wait()


def spread(tree, full, mine, back, mult, price, load, limit, nodes):
    scen, slots, count = mult.shape
    pieces = 4
    vmem = pl.BlockSpec(memory_space=pltpu.VMEM)
    hbm = pl.BlockSpec(memory_space=pltpu.HBM)
    dma = pltpu.SemaphoreType.DMA
    return pl.pallas_call(
        functools.partial(spread_kernel, nodes),
        in_specs=[pl.BlockSpec(memory_space=pltpu.SMEM)] + [vmem] * 7,
        out_specs=[hbm] * 3,
        out_shape=[
            jax.ShapeDtypeStruct(mult.shape, F32),
            jax.ShapeDtypeStruct(mult.shape, F32),
            jax.ShapeDtypeStruct(price.shape, F32),
        ],
        scratch_shapes=[
            pltpu.VMEM((nodes, slots // 4, count), F32),
            pltpu.VMEM(mult.shape, F32),
            pltpu.VMEM(price.shape, F32),
            dma((pieces, 2)), dma((pieces,)), dma(()),
        ],
        compiler_params=pltpu.CompilerParams(vmem_limit_bytes=24 * 2**20),
        name="spread",
    )(tree, full, mine, back, mult, price, load, limit)


def per_device(
    demand,
    tariff,
    feeder_price,
    multiplier,
    previous_mean,
    inverse,
    power_limit,
    weights,
    tree_node,
    building_feeder,
    feeder_limit,
):
    scen_size = lax.axis_size("scen")
    scen, count, slots = demand.shape
    nodes = 1 + COARSE + scen_size * scen // 8
    groups = 2
    rows = round_up((nodes + 1) // 2 * (slots // 4) + round_up(nodes, 8), 8 * (scen_size // 2))

    def turned(value):
        return jnp.transpose(value, (0, 2, 1))

    limit = jnp.transpose(power_limit, (1, 0))
    mult = turned(multiplier)
    mine, back, full, total = solve(
        turned(demand), mult, turned(previous_mean), jnp.transpose(inverse, (1, 2, 0)), tariff, feeder_price,
        limit, building_feeder.reshape(1, count), weights.reshape(1, scen), tree_node, nodes, groups, rows,
    )
    plan, new_multiplier, new_price = spread(
        tree_node, full, mine, back, mult, feeder_price, total.reshape(feeder_price.shape), feeder_limit, nodes
    )
    return turned(plan), turned(new_multiplier), new_price


def solution(mesh):
    in_specs = (
        P("scen", "bldg", None),
        P("scen", None),
        P("scen", None, None),
        P("scen", "bldg", None),
        P("scen", "bldg", None),
        P("bldg", None, None),
        P("bldg", None),
        P("scen"),
        P(None, "scen"),
        P("bldg"),
        P(),
    )
    out_specs = (P("scen", "bldg", None), P("scen", "bldg", None), P("scen", None, None))
    return jax.shard_map(
        per_device, mesh=mesh, in_specs=in_specs, out_specs=out_specs, check_vma=False
    )
```
